512 devices in a mesh: cell: 64 (over z, x, y_lo), aux: 8 (over y_hi, core).
Axes of the slice: x: 4, y: 8 (y_hi: 4, y_lo: 2; y = y_hi * 2 + y_lo), z: 8, core: 2. Of those that a mesh axis runs over, the one named last changes fastest.
Arguments:
- blocks: float32 [64, 32, 300, 300], P('cell', 'aux'), may hold values from -0.75 to 0.75
- cell_offsets: int32 [3, 64], replicated, may hold values from -2 to 1, as said below
- occ_coeff: float32 [2, 300, 60], replicated, may hold values from -0.25 to 0.25
- vir_coeff: float32 [64, 2, 300, 240], P('cell', None, None, 'aux'), may hold values from -0.25 to 0.25
- transfer_index: int32 [64], replicated, may hold values from 0 to 63, as said below
Outputs:
- pair_ints: float32 [2, 32, 64, 14400], P(None, 'aux', None, 'cell')
The draws below stay inside these ranges and needn't reach their ends.
Inputs may be any that keep to these rules, and one draw needn't show every extreme that they name: `cell_offsets`: column R is the integer lattice vector of cell R; the columns are the 64 cells of the centred 4 x 4 x 4 supercell, each once, in an order drawn from the seed. `transfer_index`: entry k is the index (a 4 + b) * 4 + c of the k-point k - k1 folded into the 4 x 4 x 4 mesh, for one k1 drawn from the seed; every index appears once.
All inputs are finite; a program needn't handle non-finite values.
Results may differ from the reference program's by a relative error of at most 0.00007.
Values sent between devices are 32-bit elements; how exact they have to be, the bound alone decides.
A program may use at most 64 MiB of HBM per device.

```python
import math
import jax
import jax.numpy as jnp
from jax import lax

NB = 300
NO = 60
NV = 240
KX = 4
KY = 4
NCELLS = 64
KZ = 4
NAUXS = 32


def draw_cell_offsets(key, part):
    order = jax.random.permutation(key, NCELLS).astype(jnp.int32)
    first = order // (KY * KZ) - KX // 2
    second = order // KZ % KY - KY // 2
    third = order % KZ - KZ // 2
    return jnp.stack([first, second, third]).astype(jnp.int32)


def draw_transfer_index(key, part):
    anchor = jax.random.randint(key, (), 0, NCELLS).astype(jnp.int32)
    points = jnp.arange(NCELLS, dtype=jnp.int32)
    along_a = (points // (KY * KZ) - anchor // (KY * KZ)) % KX
    along_b = (points // KZ % KY - anchor // KZ % KY) % KY
    along_c = (points % KZ - anchor % KZ) % KZ
    return ((along_a * KY + along_b) * KZ + along_c).astype(jnp.int32)


def levels(own_key, extent, pieces, low, high):
    def one(axis_at, shards_of):
        draws = jax.random.uniform(jax.random.fold_in(jax.random.fold_in(own_key, 6), axis_at), (shards_of,), jnp.float32, low / len(pieces), high / len(pieces))
        return jnp.repeat(jnp.exp(draws), extent[axis_at] // shards_of).reshape((-1,) + (1,) * (len(extent) - axis_at - 1))

    loudness = one(*pieces[0])
    for cut in pieces[1:]:
        loudness = loudness * one(*cut)
    return loudness


def normal_values(stream_key, extent, scale, limit, split=(), kind=jnp.bfloat16):
    values = scale * jax.random.normal(stream_key, extent, jnp.float32)
    if split:
        values = values * levels(stream_key, extent, split, -0.22, 0.18)
    return jnp.clip(values, -limit, limit).astype(kind)


def setup_inputs(seed: int = 0) -> dict:
    seeds = jax.random.split(jax.random.key(seed), 6)
    blocks = normal_values(seeds[0], (NCELLS, NAUXS, NB, NB), 0.125, 0.75, ((0, 64), (1, 8)), jnp.float32)
    cell_offsets = draw_cell_offsets(jax.random.fold_in(seeds[5], 71), 0)
    occ_coeff = normal_values(seeds[2], (2, NB, NO), (2 * NB) ** -0.5, 0.25, (), jnp.float32)
    vir_coeff = normal_values(seeds[3], (NCELLS, 2, NB, NV), (2 * NB) ** -0.5, 0.25, ((0, 64), (3, 8)), jnp.float32)
    transfer_index = draw_transfer_index(jax.random.fold_in(seeds[5], 71), 0)
    return {"blocks": blocks, "cell_offsets": cell_offsets, "occ_coeff": occ_coeff, "vir_coeff": vir_coeff, "transfer_index": transfer_index}


def phases(cell_offsets):
    points = jnp.arange(NCELLS, dtype=jnp.int32)
    along_a = points // (KY * KZ)
    along_b = (points // KZ) % KY
    along_c = points % KZ
    turns = (along_a[:, None] * cell_offsets[0][None, :] * (KY * KZ)
             + along_b[:, None] * cell_offsets[1][None, :] * (KX * KZ)
             + along_c[:, None] * cell_offsets[2][None, :] * (KX * KY)) % NCELLS
    angles = (2.0 * math.pi / NCELLS) * turns.astype(jnp.float32)
    return jnp.cos(angles), jnp.sin(angles)


def reference(blocks, cell_offsets, occ_coeff, vir_coeff, transfer_index):
    cosines, sines = phases(cell_offsets)
    occ_real, occ_imag = occ_coeff[0], occ_coeff[1]
    vir_real, vir_imag = vir_coeff[:, 0], vir_coeff[:, 1]
    highest = lax.Precision.HIGHEST

    def one_function(position):
        slab_blocks = lax.dynamic_index_in_dim(blocks, position, 1, keepdims=False).reshape(NCELLS, NB * NB)
        grid_real = jnp.dot(cosines, slab_blocks, precision=highest, preferred_element_type=jnp.float32).reshape(NCELLS, NB, NB)
        grid_imag = jnp.dot(sines, slab_blocks, precision=highest, preferred_element_type=jnp.float32).reshape(NCELLS, NB, NB)
        half_real = jnp.einsum("mi,kmn->kin", occ_real, grid_real, precision=highest) + jnp.einsum("mi,kmn->kin", occ_imag, grid_imag, precision=highest)
        half_imag = jnp.einsum("mi,kmn->kin", occ_real, grid_imag, precision=highest) - jnp.einsum("mi,kmn->kin", occ_imag, grid_real, precision=highest)
        band_real = jnp.einsum("kin,kna->kia", half_real, vir_real, precision=highest) - jnp.einsum("kin,kna->kia", half_imag, vir_imag, precision=highest)
        band_imag = jnp.einsum("kin,kna->kia", half_real, vir_imag, precision=highest) + jnp.einsum("kin,kna->kia", half_imag, vir_real, precision=highest)
        return jnp.stack([band_real, band_imag])

    banded = lax.map(one_function, jnp.arange(NAUXS, dtype=jnp.int32))
    source = jnp.argsort(transfer_index).astype(jnp.int32)
    regrouped = jnp.take(banded, source, axis=2)
    return jnp.transpose(regrouped.reshape(NAUXS, 2, NCELLS, NO * NV), (1, 0, 2, 3))
```

```python
import functools

import jax
import jax.numpy as jnp
from jax import lax
from jax.experimental import pallas as pl
from jax.experimental.pallas import tpu as pltpu
from jax.sharding import PartitionSpec as P

CELLS = 64
AUX = 8
NB = 300
NO = 60
NV = 240
ROWS = 4
LANES = 128
TILES = 3
GROUP = 16
WORKERS = 60
PAIRS = 225
MESH = pl.DeviceIdType.MESH
F32 = jnp.float32
BF16 = jnp.bfloat16


def split(x):
    high = x.astype(BF16)
    low = (x - high.astype(F32)).astype(BF16)
    return high, low


def dot(a, b, transposed=False):
    dims = (((1,), (1 if transposed else 0,)), ((), ()))
    return lax.dot_general(a, b, dims, preferred_element_type=F32)


def dot3(a, b, transposed=False):
    return (
        dot(a[0], b[0], transposed)
        + dot(a[0], b[1], transposed)
        + dot(a[1], b[0], transposed)
    )


def tile_lanes(tile):
    return LANES if tile < TILES - 1 else NB - LANES * (TILES - 1)


def quarter_turns():
    row = lax.broadcasted_iota(jnp.int32, (8, LANES), 0)
    return jnp.where(row < ROWS, -1.0, 1.0).astype(F32)


def times_i(x, sign):
    return pltpu.roll(x, ROWS, 0) * sign


def four_points(x, sign):
    even, odd = x[0] + x[2], x[1] + x[3]
    left, right = x[0] - x[2], times_i(x[1] - x[3], sign)
    return even + odd, left + right, even - odd, left - right


def kernel(
    pos, blocks, occ, vir, out,
    occ_v, blocks_v, sent_half, got_half_0, got_half_1, got_half_2, middle, sent_spec, got_spec,
    vir_own, vir_all, vir_rows, vir_high, vir_low, band, sent_pairs,
    load_sem, vir_load_sem, half_send, half_recv, half_local, spec_send, spec_recv, spec_local,
    pair_send, pair_recv, pair_local, vir_send, vir_recv, vir_local,
):
    got_half = (got_half_0, got_half_1, got_half_2)
    me = lax.axis_index("cell")
    my_aux = lax.axis_index("aux")
    active = lax.rem(me, GROUP) != GROUP - 1
    my_slot = me - me // GROUP

    barrier = pltpu.get_barrier_semaphore()

    def greet(j, carry):
        pl.semaphore_signal(
            barrier, inc=1, device_id={"cell": lax.rem(me + j, CELLS)}, device_id_type=MESH
        )
        return carry

    lax.fori_loop(1, CELLS, greet, 0)

    def greet_aux(j, carry):
        pl.semaphore_signal(
            barrier, inc=1, device_id={"aux": lax.rem(my_aux + j, AUX)}, device_id_type=MESH
        )
        return carry

    lax.fori_loop(1, AUX, greet_aux, 0)

    occ_loads = [pltpu.make_async_copy(occ.at[:, t, :], occ_v.at[t], load_sem.at[t]) for t in range(2)]
    block_loads = [pltpu.make_async_copy(blocks.at[:, p, :], blocks_v.at[p], load_sem.at[2 + p]) for p in range(ROWS)]
    for load in occ_loads + block_loads:
        load.start()
    vir_load = pltpu.make_async_copy(vir, vir_own, vir_load_sem)
    vir_load.start()

    for load in occ_loads:
        load.wait()
    blank = jnp.zeros((64 - NO, NB), F32)
    left_rows = jnp.concatenate([occ_v[0], blank, -occ_v[1], blank], axis=0)
    left = split(left_rows)
    for load in block_loads:
        load.wait()

    def half_product(tile):
        width = tile_lanes(tile)
        for pair in range(ROWS // 2):
            parts = []
            for p in (2 * pair, 2 * pair + 1):
                part = blocks_v[p, :, tile * LANES : tile * LANES + width]
                if width < LANES:
                    part = jnp.concatenate([part, jnp.zeros((NB, LANES - width), F32)], axis=1)
                parts.append(part)
            product = dot3(left, split(jnp.concatenate(parts, axis=1)))
            for at in range(2):
                for t in range(2):
                    rows = product[t * 64 : t * 64 + NO, at * LANES : (at + 1) * LANES]
                    sent_half[tile, pl.ds(t * ROWS + 2 * pair + at, NO, stride=8), :] = rows

    def send_half(tile):
        def one(j, carry):
            peer = lax.rem(me + j, CELLS)
            slot = peer - peer // GROUP

            @pl.when(lax.rem(peer, GROUP) != GROUP - 1)
            def _():
                pltpu.make_async_remote_copy(
                    src_ref=sent_half.at[tile, pl.ds(pl.multiple_of(slot * 8, 8), 8)],
                    dst_ref=got_half[tile].at[me],
                    send_sem=half_send.at[tile],
                    recv_sem=half_recv.at[tile],
                    device_id={"cell": peer},
                    device_id_type=MESH,
                ).start()

            return carry

        lax.fori_loop(1, CELLS, one, 0)

        @pl.when(active)
        def _():
            pltpu.make_async_copy(
                sent_half.at[tile, pl.ds(pl.multiple_of(my_slot * 8, 8), 8)], got_half[tile].at[me], half_local.at[tile]
            ).start()

    half_product(0)
    pl.semaphore_wait(barrier, CELLS - 1 + AUX - 1)
    send_half(0)
    for tile in range(1, TILES):
        half_product(tile)
        send_half(tile)

    vir_load.wait()

    def send_vir(j, carry):
        pltpu.make_async_remote_copy(
            src_ref=vir_own,
            dst_ref=vir_all.at[pl.ds(my_aux * (NV // AUX), NV // AUX)],
            send_sem=vir_send,
            recv_sem=vir_recv,
            device_id={"aux": lax.rem(my_aux + j, AUX)},
            device_id_type=MESH,
        ).start()
        return carry

    lax.fori_loop(1, AUX, send_vir, 0)
    own_vir = pltpu.make_async_copy(vir_own, vir_all.at[pl.ds(my_aux * (NV // AUX), NV // AUX)], vir_local)
    own_vir.start()

    sign = quarter_turns()

    def wait_bytes(ref, sem):
        pltpu.make_async_copy(ref, ref, sem).wait()

    def fourier(tile):
        wait_bytes(got_half[tile].at[pl.ds(0, CELLS - 1)], half_recv.at[tile])
        wait_bytes(got_half[tile].at[0], half_local.at[tile])
        for c in range(4):
            x = [[got_half[tile][pos[a * 16 + b * 4 + c]] for b in range(4)] for a in range(4)]
            columns = [four_points([x[a][b] for a in range(4)], sign) for b in range(4)]
            for a in range(4):
                y = four_points([columns[b][a] for b in range(4)], sign)
                for b in range(4):
                    middle[a * 16 + b * 4 + c] = y[b]
        for at in range(16):
            y = four_points([middle[at * 4 + c] for c in range(4)], sign)
            for c in range(4):
                sent_spec[tile, at * 4 + c] = y[c]

        def one(j, carry):
            peer = lax.rem(me + j, CELLS)
            pltpu.make_async_remote_copy(
                src_ref=sent_spec.at[tile, peer],
                dst_ref=got_spec.at[tile, my_slot],
                send_sem=spec_send.at[tile],
                recv_sem=spec_recv.at[tile],
                device_id={"cell": peer},
                device_id_type=MESH,
            ).start()
            return carry

        lax.fori_loop(1, CELLS, one, 0)
        pltpu.make_async_copy(sent_spec.at[tile, me], got_spec.at[tile, my_slot], spec_local.at[tile]).start()

    @pl.when(active)
    def _():
        for tile in range(TILES):
            fourier(tile)

    own_vir.wait()
    wait_bytes(vir_all.at[pl.ds(0, NV - NV // AUX)], vir_recv)
    spread = [pltpu.make_async_copy(vir_all.at[:, t, :], vir_rows.at[t], load_sem.at[t]) for t in range(2)]
    for copy in spread:
        copy.start()
    for copy in spread:
        copy.wait()
    for tile in range(TILES):
        width = tile_lanes(tile)
        for t in range(2):
            part = vir_rows[t, :, tile * LANES : tile * LANES + width]
            if width < LANES:
                part = jnp.concatenate([part, jnp.zeros((NV, LANES - width), F32)], axis=1)
            high, low = split(part)
            vir_high[tile, :, t * LANES : (t + 1) * LANES] = high
            vir_low[tile, :, t * LANES : (t + 1) * LANES] = low

    per_group = WORKERS // 4

    def wait_spec(tile):
        @pl.when(active)
        def _():
            wait_bytes(got_spec.at[tile, pl.ds(0, WORKERS - 1)], spec_recv.at[tile])
            wait_bytes(got_spec.at[tile, 0], spec_local.at[tile])

        @pl.when(jnp.logical_not(active))
        def _():
            wait_bytes(got_spec.at[tile, pl.ds(0, WORKERS)], spec_recv.at[tile])

    def partial_band(tile, group):
        x = got_spec[tile, pl.ds(group * per_group, per_group)]
        turned = jnp.stack([times_i(x[n], sign) for n in range(per_group)])
        both = jnp.concatenate([x.reshape(per_group * 8, LANES), turned.reshape(per_group * 8, LANES)], axis=1)
        return dot3(split(both), (vir_high[tile], vir_low[tile]), transposed=True)

    rows_per_group = per_group * 8
    for tile in range(TILES - 1):
        wait_spec(tile)

        def accumulate(group, carry):
            at = pl.ds(pl.multiple_of(group * rows_per_group, 8), rows_per_group)
            value = partial_band(tile, group)
            if tile:
                value = band[at, :] + value
            band[at, :] = value
            return carry

        lax.fori_loop(0, 4, accumulate, 0)

    wait_spec(TILES - 1)
    lane = lax.broadcasted_iota(jnp.int32, (8, 2 * LANES), 1)

    def finish(group, carry):
        at = pl.ds(pl.multiple_of(group * rows_per_group, 8), rows_per_group)
        value = band[at, :] + partial_band(TILES - 1, group)
        wide = jnp.concatenate([value, jnp.zeros((rows_per_group, 2 * LANES - NV), F32)], axis=1)
        wide = wide.reshape(per_group, 8, 2 * LANES)
        for m in range(GROUP):
            shift = (NV - PAIRS) * m
            if m == 0:
                chunk = wide[0]
            else:
                chunk = pltpu.roll(wide[m - 1], 2 * LANES - (NV - shift), 1)
                if m < GROUP - 1:
                    chunk = jnp.where(lane < shift, chunk, pltpu.roll(wide[m], shift, 1))
            sent_pairs[group * GROUP + m] = chunk

        def one(m, inner):
            peer = group * GROUP + m

            @pl.when(peer != me)
            def _():
                pltpu.make_async_remote_copy(
                    src_ref=sent_pairs.at[peer],
                    dst_ref=out.at[me],
                    send_sem=pair_send,
                    recv_sem=pair_recv,
                    device_id={"cell": peer},
                    device_id_type=MESH,
                ).start()

            @pl.when(peer == me)
            def _():
                pltpu.make_async_copy(sent_pairs.at[peer], out.at[peer], pair_local).start()

            return inner

        lax.fori_loop(0, GROUP, one, 0)
        return carry

    lax.fori_loop(0, 4, finish, 0)

    for tile in range(TILES):
        @pl.when(active)
        def _():
            wait_bytes(sent_half.at[tile, pl.ds(0, (WORKERS - 1) * 8)], half_send.at[tile])
            wait_bytes(sent_spec.at[tile, pl.ds(0, CELLS - 1)], spec_send.at[tile])

        @pl.when(jnp.logical_not(active))
        def _():
            wait_bytes(sent_half.at[tile], half_send.at[tile])

    wait_bytes(vir_all.at[pl.ds(0, NV - NV // AUX)], vir_send)
    wait_bytes(sent_pairs.at[pl.ds(0, CELLS - 1)], pair_send)
    wait_bytes(out.at[0], pair_local)
    wait_bytes(out.at[pl.ds(0, CELLS - 1)], pair_recv)


def exchange(pos, blocks, occ, vir):
    dma = pltpu.SemaphoreType.DMA
    return pl.pallas_call(
        kernel,
        out_shape=jax.ShapeDtypeStruct((CELLS, 8, 2 * LANES), F32),
        in_specs=[
            pl.BlockSpec(memory_space=pltpu.SMEM),
            pl.BlockSpec(memory_space=pl.ANY),
            pl.BlockSpec(memory_space=pl.ANY),
            pl.BlockSpec(memory_space=pl.ANY),
        ],
        out_specs=pl.BlockSpec(memory_space=pltpu.VMEM),
        scratch_shapes=[
            pltpu.VMEM((2, NO, NB), F32),
            pltpu.VMEM((ROWS, NB, NB), F32),
            pltpu.VMEM((TILES, WORKERS * 8, LANES), F32),
            pltpu.VMEM((CELLS, 8, LANES), F32),
            pltpu.VMEM((CELLS, 8, LANES), F32),
            pltpu.VMEM((CELLS, 8, LANES), F32),
            pltpu.VMEM((CELLS, 8, LANES), F32),
            pltpu.VMEM((TILES, CELLS, 8, LANES), F32),
            pltpu.VMEM((TILES, WORKERS, 8, LANES), F32),
            pltpu.VMEM((NV // AUX, 2, NB), F32),
            pltpu.VMEM((NV, 2, NB), F32),
            pltpu.VMEM((2, NV, NB), F32),
            pltpu.VMEM((TILES, NV, 2 * LANES), BF16),
            pltpu.VMEM((TILES, NV, 2 * LANES), BF16),
            pltpu.VMEM((WORKERS * 8, NV), F32),
            pltpu.VMEM((CELLS, 8, 2 * LANES), F32),
            dma((2 + ROWS,)),
            dma,
            dma((TILES,)),
            dma((TILES,)),
            dma((TILES,)),
            dma((TILES,)),
            dma((TILES,)),
            dma((TILES,)),
            dma,
            dma,
            dma,
            dma,
            dma,
            dma,
        ],
        compiler_params=pltpu.CompilerParams(
            collective_id=0, has_side_effects=True, vmem_limit_bytes=63 << 20
        ),
        name="transform",
    )(pos, blocks, occ, vir)


def inverse(order):
    index = jnp.arange(CELLS, dtype=jnp.int32)
    return jnp.sum(jnp.where(order[None, :] == index[:, None], index[None, :], 0), axis=1)


def on_device(blocks, cell_offsets, occ_coeff, vir_coeff, transfer_index):
    folded = cell_offsets & 3
    pos = inverse(folded[0] * 16 + folded[1] * 4 + folded[2])
    got = exchange(
        pos,
        jnp.transpose(blocks[0], (1, 0, 2)),
        jnp.transpose(occ_coeff, (2, 0, 1)),
        jnp.transpose(vir_coeff[0], (2, 0, 1)),
    )
    source = inverse(transfer_index)
    ordered = jnp.take(got, source, axis=0)[:, :, :PAIRS]
    return jnp.transpose(ordered.reshape(CELLS, 2, ROWS, PAIRS), (1, 2, 0, 3))


def solution(mesh):
    placed = (P("cell", "aux", None, None), P(), P(), P("cell", None, None, "aux"), P())
    return jax.shard_map(
        on_device,
        mesh=mesh,
        in_specs=placed,
        out_specs=P(None, "aux", None, "cell"),
        check_vma=False,
    )
```

```python
import functools

import jax
import jax.numpy as jnp
from jax import lax
from jax.experimental import pallas as pl
from jax.experimental.pallas import tpu as pltpu
from jax.sharding import PartitionSpec as P

CELLS = 64
AUX = 8
NB = 300
NO = 60
NV = 240
PIECE = NV // AUX
ROWS = 4
LANES = 128
WIDE = 2 * LANES
REST = NB - WIDE
HALF = LANES // 2
GROUP = 16
WORKERS = 60
PAIRS = 225
SLOTS = 64
FIRST, SMALL, SECOND = 0, 1, 2
MESH = pl.DeviceIdType.MESH
F32 = jnp.float32
BF16 = jnp.bfloat16


def split(x):
    high = x.astype(BF16)
    low = (x - high.astype(F32)).astype(BF16)
    return high, low


def dot(a, b, transposed=False):
    dims = (((1,), (1 if transposed else 0,)), ((), ()))
    return lax.dot_general(a, b, dims, preferred_element_type=F32)


def dot3(a, b, transposed=False):
    return (
        dot(a[0], b[0], transposed)
        + dot(a[0], b[1], transposed)
        + dot(a[1], b[0], transposed)
    )


def times_i(x, sign):
    return pltpu.roll(x, ROWS, 0) * sign


def four_points(x, sign):
    even, odd = x[0] + x[2], x[1] + x[3]
    left, right = x[0] - x[2], times_i(x[1] - x[3], sign)
    return even + odd, left + right, even - odd, left - right


def four_complex(x):
    def add(a, b):
        return a[0] + b[0], a[1] + b[1]

    def sub(a, b):
        return a[0] - b[0], a[1] - b[1]

    even, odd = add(x[0], x[2]), add(x[1], x[3])
    left, across = sub(x[0], x[2]), sub(x[1], x[3])
    return (
        add(even, odd),
        (left[0] - across[1], left[1] + across[0]),
        sub(even, odd),
        (left[0] + across[1], left[1] - across[0]),
    )


def wait_bytes(ref, sem):
    pltpu.make_async_copy(ref, ref, sem).wait()


def kernel(
    cells, blocks, occ, vir, out_0, out_1,
    cells_v, occ_v, blocks_v, pos_v, pos_s,
    sent_half_0, sent_half_1, sent_rest, got_half_0, got_half_1, got_rest,
    middle, middle_rest, sent_spec, sent_spec_rest, got_spec_0, got_spec_1, got_spec_rest,
    vir_own, vir_all, vir_rows, vir_high, vir_low, rest_high, rest_low, band, sent_pairs,
    load_sem, pos_sem, half_send, half_recv, half_local, spec_send, spec_recv, spec_local,
    pair_send, pair_recv, pair_local, vir_load_sem, vir_send, vir_recv, vir_local,
):
    me = lax.axis_index("cell")
    my_aux = lax.axis_index("aux")
    partner = my_aux + 1 - 2 * lax.rem(my_aux, 2)
    active = lax.rem(me, GROUP) != GROUP - 1
    my_slot = me - me // GROUP
    out = (out_0, out_1)
    sent_half = (sent_half_0, sent_rest, sent_half_1)
    got_half = (got_half_0, got_rest, got_half_1)
    got_spec = (got_spec_0, got_spec_rest, got_spec_1)

    barrier = pltpu.get_barrier_semaphore()

    def greet(j, carry):
        pl.semaphore_signal(
            barrier, inc=1, device_id={"cell": lax.rem(me + j, CELLS)}, device_id_type=MESH
        )
        return carry

    def greet_aux(j, carry):
        pl.semaphore_signal(
            barrier, inc=1, device_id={"aux": lax.rem(my_aux + 2 * j, AUX)}, device_id_type=MESH
        )
        return carry

    lax.fori_loop(1, CELLS, greet, 0)
    lax.fori_loop(1, AUX // 2, greet_aux, 0)
    pl.semaphore_signal(barrier, inc=1, device_id={"aux": partner}, device_id_type=MESH)

    occ_loads = [pltpu.make_async_copy(occ.at[:, t, :], occ_v.at[t], load_sem.at[t]) for t in range(2)]
    block_loads = [pltpu.make_async_copy(blocks.at[:, p, :], blocks_v.at[p], load_sem.at[2 + p]) for p in range(ROWS)]
    vir_load = pltpu.make_async_copy(vir, vir_own, vir_load_sem)
    cells_load = pltpu.make_async_copy(cells, cells_v, pos_sem)
    cells_load.start()
    for load in occ_loads + block_loads:
        load.start()
    vir_load.start()
    cells_load.wait()

    folded = cells_v[...] & 3
    number = folded[0:1] * 16 + folded[1:2] * 4 + folded[2:3]
    wanted = lax.broadcasted_iota(jnp.int32, (CELLS, CELLS), 0)
    holder = lax.broadcasted_iota(jnp.int32, (CELLS, CELLS), 1)
    found = jnp.sum(jnp.where(number == wanted, holder, 0), axis=1, keepdims=True)
    pos_v[...] = jnp.broadcast_to(found & (CELLS - 1), (CELLS, LANES))
    pos_copy = pltpu.make_async_copy(pos_v, pos_s, pos_sem)
    pos_copy.start()

    for load in occ_loads:
        load.wait()
    blank = jnp.zeros((SLOTS - NO, NB), F32)
    left = split(jnp.concatenate([occ_v[0], blank, -occ_v[1], blank], axis=0))

    def half_product(pair):
        for p in (2 * pair, 2 * pair + 1):
            block_loads[p].wait()
        for at in range(2):
            product = dot3(left, split(blocks_v[2 * pair + at, :, 0:WIDE]))
            for t in range(2):
                for n in range(2):
                    rows = product[t * SLOTS : t * SLOTS + NO, n * LANES : (n + 1) * LANES]
                    sent_half[2 * pair][pl.ds(t * 4 + n * 2 + at, NO, stride=8), :] = rows

    def rest_product():
        gap = jnp.zeros((NB, HALF - REST), F32)
        parts = []
        for at in range(2):
            for pair in range(2):
                parts += [blocks_v[2 * pair + at, :, WIDE:NB], gap]
        product = dot3(left, split(jnp.concatenate(parts, axis=1)))
        for t in range(2):
            for at in range(2):
                sent_rest[:, t * 2 + at, :] = product[t * SLOTS : t * SLOTS + NO, at * LANES : (at + 1) * LANES]

    def half_source(part, slot):
        if part == SMALL:
            return sent_rest.at[slot]
        return sent_half[part].at[pl.ds(pl.multiple_of(slot * 8, 8), 8)]

    def send_half(part):
        def one(j, carry):
            peer = lax.rem(me + j, CELLS)

            @pl.when(lax.rem(peer, GROUP) != GROUP - 1)
            def _():
                pltpu.make_async_remote_copy(
                    src_ref=half_source(part, peer - peer // GROUP),
                    dst_ref=got_half[part].at[me],
                    send_sem=half_send.at[part],
                    recv_sem=half_recv.at[part],
                    device_id={"cell": peer},
                    device_id_type=MESH,
                ).start()

            return carry

        lax.fori_loop(1, CELLS, one, 0)

        @pl.when(active)
        def _():
            pltpu.make_async_copy(half_source(part, my_slot), got_half[part].at[me], half_local.at[part]).start()

    half_product(0)
    pl.semaphore_wait(barrier, CELLS - 1 + AUX // 2)
    send_half(FIRST)

    def vir_slot(aux):
        return vir_all.at[pl.ds(aux * PIECE, PIECE)]

    def vir_copy(source, aux, target, sem):
        return pltpu.make_async_remote_copy(
            src_ref=source,
            dst_ref=vir_slot(aux),
            send_sem=vir_send.at[sem],
            recv_sem=vir_recv.at[sem],
            device_id={"aux": target},
            device_id_type=MESH,
        )

    vir_load.wait()

    def send_vir(j, carry):
        vir_copy(vir_own, my_aux, lax.rem(my_aux + 2 * j, AUX), 0).start()
        return carry

    lax.fori_loop(1, AUX // 2, send_vir, 0)
    vir_copy(vir_own, my_aux, partner, 1).start()
    own_vir = pltpu.make_async_copy(vir_own, vir_slot(my_aux), vir_local)
    own_vir.start()

    half_product(1)
    rest_product()
    send_half(SMALL)
    send_half(SECOND)

    pos_copy.wait()
    sign = jnp.where(lax.broadcasted_iota(jnp.int32, (8, LANES), 0) < ROWS, -1.0, 1.0).astype(F32)

    def spec_target(part):
        if part == SMALL:
            return got_spec_rest.at[my_slot]
        return got_spec[part].at[pl.ds(pl.multiple_of(my_slot * 8, 8), 8)]

    def spec_source(part, peer):
        if part == SMALL:
            return sent_spec_rest.at[peer]
        return sent_spec.at[part // 2, peer]

    def arrived_half(part):
        wait_bytes(got_half[part].at[pl.ds(0, CELLS - 1)], half_recv.at[part])
        wait_bytes(got_half[part].at[0], half_local.at[part])

    def send_spec(part):
        def one(j, carry):
            peer = lax.rem(me + j, CELLS)
            pltpu.make_async_remote_copy(
                src_ref=spec_source(part, peer),
                dst_ref=spec_target(part),
                send_sem=spec_send.at[part],
                recv_sem=spec_recv.at[part],
                device_id={"cell": peer},
                device_id_type=MESH,
            ).start()
            return carry

        lax.fori_loop(1, CELLS, one, 0)
        pltpu.make_async_copy(spec_source(part, me), spec_target(part), spec_local.at[part]).start()

    def fourier(part):
        arrived_half(part)
        for c in range(4):
            x = [[got_half[part][pos_s[a * 16 + b * 4 + c, 0]] for b in range(4)] for a in range(4)]
            columns = [four_points([x[a][b] for a in range(4)], sign) for b in range(4)]
            for a in range(4):
                y = four_points([columns[b][a] for b in range(4)], sign)
                for b in range(4):
                    middle[a * 16 + b * 4 + c] = y[b]
        for at in range(16):
            y = four_points([middle[at * 4 + c] for c in range(4)], sign)
            for c in range(4):
                sent_spec[part // 2, at * 4 + c] = y[c]
        send_spec(part)

    def fourier_rest():
        arrived_half(SMALL)
        for c in range(4):
            x = [[None] * 4 for _ in range(4)]
            for a in range(4):
                for b in range(4):
                    both = got_rest[pos_s[a * 16 + b * 4 + c, 0]]
                    x[a][b] = (both[0:2], both[2:4])
            columns = [four_complex([x[a][b] for a in range(4)]) for b in range(4)]
            for a in range(4):
                y = four_complex([columns[b][a] for b in range(4)])
                for b in range(4):
                    for t in range(2):
                        middle_rest[a * 16 + b * 4 + c, 2 * t : 2 * t + 2] = y[b][t]
        for at in range(16):
            x = [(middle_rest[at * 4 + c, 0:2], middle_rest[at * 4 + c, 2:4]) for c in range(4)]
            y = four_complex(x)
            for c in range(4):
                for t in range(2):
                    sent_spec_rest[at * 4 + c, 2 * t : 2 * t + 2] = y[c][t]
        send_spec(SMALL)

    @pl.when(active)
    def _():
        fourier(FIRST)

    wait_bytes(vir_all.at[pl.ds(0, NV // 2 - PIECE)], vir_recv.at[0])

    def hand_on(j, carry):
        source = lax.rem(my_aux + 2 * j, AUX)
        vir_copy(vir_slot(source), source, partner, 1).start()
        return carry

    lax.fori_loop(1, AUX // 2, hand_on, 0)

    @pl.when(active)
    def _():
        fourier_rest()
        fourier(SECOND)

    own_vir.wait()
    wait_bytes(vir_all.at[pl.ds(0, NV // 2)], vir_recv.at[1])
    spread = [pltpu.make_async_copy(vir_all.at[:, t, :], vir_rows.at[t], load_sem.at[t]) for t in range(2)]
    for copy in spread:
        copy.start()
    for copy in spread:
        copy.wait()
    gap = jnp.zeros((NV, HALF - REST), F32)
    none = jnp.zeros((NV, HALF), F32)
    for t in range(2):
        high, low = split(vir_rows[t, :, 0:WIDE])
        vir_high[:, t * WIDE : (t + 1) * WIDE] = high
        vir_low[:, t * WIDE : (t + 1) * WIDE] = low
        small = jnp.concatenate([vir_rows[t, :, WIDE:NB], gap], axis=1)
        for g in range(2):
            placed = jnp.concatenate([none, small] if g else [small, none], axis=1)
            high, low = split(placed)
            rest_high[g, :, t * LANES : (t + 1) * LANES] = high
            rest_low[g, :, t * LANES : (t + 1) * LANES] = low

    def arrived_spec(part):
        step = 1 if part == SMALL else 8

        @pl.when(active)
        def _():
            wait_bytes(got_spec[part].at[pl.ds(0, (WORKERS - 1) * step)], spec_recv.at[part])
            wait_bytes(got_spec[part].at[pl.ds(0, step)], spec_local.at[part])

        @pl.when(jnp.logical_not(active))
        def _():
            wait_bytes(got_spec[part].at[pl.ds(0, WORKERS * step)], spec_recv.at[part])

    def turned(even, odd):
        upper = jnp.concatenate(even + [-x for x in odd], axis=1)
        lower = jnp.concatenate(odd + even, axis=1)
        return [upper, lower]

    lane = lax.broadcasted_iota(jnp.int32, (ROWS, WIDE), 1)

    def band_and_pairs(g):
        part = 2 * g
        arrived_spec(part)
        if g == 0:
            arrived_spec(SMALL)
        main, small = [], []
        for at in range(2):
            x = [[got_spec[part][pl.ds(t * 4 + n * 2 + at, SLOTS, stride=8), :] for n in range(2)] for t in range(2)]
            main += turned(x[0], x[1])
            y = [got_spec_rest[:, t * 2 + at, :] for t in range(2)]
            small += turned([y[0]], [y[1]])
        value = dot3(split(jnp.concatenate(main, axis=0)), (vir_high[...], vir_low[...]), transposed=True)
        value = value + dot3(split(jnp.concatenate(small, axis=0)), (rest_high[g], rest_low[g]), transposed=True)
        value = jnp.concatenate([value, jnp.zeros((4 * SLOTS, WIDE - NV), F32)], axis=1)
        for at in range(2):
            for t in range(2):
                start = (at * 2 + t) * SLOTS
                for n in range(2):
                    band[g, n, pl.ds(t * 2 + at, NO, stride=4), :] = value[start : start + NO, n * LANES : (n + 1) * LANES]

        def wide(i):
            return jnp.concatenate([band[g, n, 4 * i : 4 * i + 4, :] for n in range(2)], axis=1)

        for block in range(4):
            base = block * (GROUP - 1)
            for m in range(GROUP):
                shift = (NV - PAIRS) * m
                if m == 0:
                    chunk = wide(base)
                else:
                    chunk = pltpu.roll(wide(base + m - 1), WIDE - (NV - shift), 1)
                    if m < GROUP - 1:
                        chunk = jnp.where(lane < shift, chunk, pltpu.roll(wide(base + m), shift, 1))
                sent_pairs[g, block * GROUP + m] = chunk

            def one(m, inner):
                peer = block * GROUP + m

                @pl.when(peer != me)
                def _():
                    pltpu.make_async_remote_copy(
                        src_ref=sent_pairs.at[g, peer],
                        dst_ref=out[g].at[me],
                        send_sem=pair_send.at[g],
                        recv_sem=pair_recv.at[g],
                        device_id={"cell": peer},
                        device_id_type=MESH,
                    ).start()

                @pl.when(peer == me)
                def _():
                    pltpu.make_async_copy(sent_pairs.at[g, peer], out[g].at[peer], pair_local.at[g]).start()

                return inner

            lax.fori_loop(0, GROUP, one, 0)

    for g in range(2):
        band_and_pairs(g)

    for part in (FIRST, SMALL, SECOND):
        step = 1 if part == SMALL else 8
        spec = sent_spec_rest if part == SMALL else sent_spec.at[part // 2]

        @pl.when(active)
        def _():
            wait_bytes(sent_half[part].at[pl.ds(0, (WORKERS - 1) * step)], half_send.at[part])
            wait_bytes(spec.at[pl.ds(0, CELLS - 1)], spec_send.at[part])

        @pl.when(jnp.logical_not(active))
        def _():
            wait_bytes(sent_half[part].at[pl.ds(0, WORKERS * step)], half_send.at[part])

    wait_bytes(vir_all.at[pl.ds(0, NV // 2 - PIECE)], vir_send.at[0])
    wait_bytes(vir_all.at[pl.ds(0, NV // 2)], vir_send.at[1])
    for g in range(2):
        wait_bytes(sent_pairs.at[g, pl.ds(0, CELLS - 1)], pair_send.at[g])
        wait_bytes(out[g].at[0], pair_local.at[g])
        wait_bytes(out[g].at[pl.ds(0, CELLS - 1)], pair_recv.at[g])


def exchange(cells, blocks, occ, vir):
    dma = pltpu.SemaphoreType.DMA
    pairs = jax.ShapeDtypeStruct((CELLS, ROWS, WIDE), F32)
    tiles = pltpu.VMEM((CELLS, 8, LANES), F32)
    halves = pltpu.VMEM((SLOTS, 4, LANES), F32)
    return pl.pallas_call(
        kernel,
        out_shape=(pairs, pairs),
        in_specs=[
            pl.BlockSpec(memory_space=pl.ANY),
            pl.BlockSpec(memory_space=pl.ANY),
            pl.BlockSpec(memory_space=pl.ANY),
            pl.BlockSpec(memory_space=pl.ANY),
        ],
        out_specs=(pl.BlockSpec(memory_space=pltpu.VMEM), pl.BlockSpec(memory_space=pltpu.VMEM)),
        scratch_shapes=[
            pltpu.VMEM((3, CELLS), jnp.int32),
            pltpu.VMEM((2, NO, NB), F32),
            pltpu.VMEM((ROWS, NB, NB), F32),
            pltpu.VMEM((CELLS, LANES), jnp.int32),
            pltpu.SMEM((CELLS, LANES), jnp.int32),
            pltpu.VMEM((WORKERS * 8, LANES), F32),
            pltpu.VMEM((WORKERS * 8, LANES), F32),
            pltpu.VMEM((WORKERS, 4, LANES), F32),
            tiles,
            tiles,
            halves,
            tiles,
            halves,
            pltpu.VMEM((2, CELLS, 8, LANES), F32),
            halves,
            pltpu.VMEM((SLOTS * 8, LANES), F32),
            pltpu.VMEM((SLOTS * 8, LANES), F32),
            halves,
            pltpu.VMEM((PIECE, 2, NB), F32),
            pltpu.VMEM((NV, 2, NB), F32),
            pltpu.VMEM((2, NV, NB), F32),
            pltpu.VMEM((NV, 2 * WIDE), BF16),
            pltpu.VMEM((NV, 2 * WIDE), BF16),
            pltpu.VMEM((2, NV, WIDE), BF16),
            pltpu.VMEM((2, NV, WIDE), BF16),
            pltpu.VMEM((2, 2, NO * 4, LANES), F32),
            pltpu.VMEM((2, CELLS, ROWS, WIDE), F32),
            dma((2 + ROWS,)),
            dma,
            dma((3,)),
            dma((3,)),
            dma((3,)),
            dma((3,)),
            dma((3,)),
            dma((3,)),
            dma((2,)),
            dma((2,)),
            dma((2,)),
            dma,
            dma((2,)),
            dma((2,)),
            dma,
        ],
        compiler_params=pltpu.CompilerParams(
            collective_id=0, has_side_effects=True, vmem_limit_bytes=44 << 20
        ),
        name="transform",
    )(cells, blocks, occ, vir)


def reorder_kernel(transfer, got_0, got_1, out, rows, ordered, sem):
    first = transfer[0]
    shifts = (first // 16, first // 4 % 4, first % 4)
    along = [[(n - shift) & 3 for n in range(4)] for shift in shifts]
    copies = []
    for g, got in enumerate((got_0, got_1)):
        for q in range(CELLS):
            source = along[0][q // 16] * 16 + along[1][q // 4 % 4] * 4 + along[2][q % 4]
            tile = got[source]
            for t in range(2):
                for n in range(2):
                    at = (t * ROWS + 2 * g) * CELLS + q
                    rows[n, pl.ds(at, 2, stride=CELLS), :] = tile[2 * t : 2 * t + 2, n * LANES : (n + 1) * LANES]
        for t in range(2):
            for p in (2 * g, 2 * g + 1):
                at = (t * ROWS + p) * CELLS
                ordered[t, p, :, 0:LANES] = rows[0, at : at + CELLS, :]
                ordered[t, p, :, LANES:PAIRS] = rows[1, at : at + CELLS, 0 : PAIRS - LANES]
            both = pl.ds(2 * g, 2)
            copy = pltpu.make_async_copy(ordered.at[t, both], out.at[t, both], sem.at[g, t])
            copy.start()
            copies.append(copy)
    for copy in copies:
        copy.wait()


def reorder(transfer, got_0, got_1):
    whole = pl.BlockSpec(memory_space=pltpu.VMEM)
    return pl.pallas_call(
        reorder_kernel,
        out_shape=jax.ShapeDtypeStruct((2, ROWS, CELLS, PAIRS), F32),
        in_specs=[pl.BlockSpec(memory_space=pltpu.SMEM), whole, whole],
        out_specs=pl.BlockSpec(memory_space=pl.ANY),
        scratch_shapes=[
            pltpu.VMEM((2, 2 * ROWS * CELLS, LANES), F32),
            pltpu.VMEM((2, ROWS, CELLS, PAIRS), F32),
            pltpu.SemaphoreType.DMA((2, 2)),
        ],
        compiler_params=pltpu.CompilerParams(vmem_limit_bytes=16 << 20),
        name="reorder",
    )(transfer, got_0, got_1)


def on_device(blocks, cell_offsets, occ_coeff, vir_coeff, transfer_index):
    keep = functools.partial(pltpu.with_memory_space_constraint, memory_space=pltpu.HBM)
    got = exchange(
        keep(cell_offsets),
        keep(jnp.transpose(blocks[0], (1, 0, 2))),
        keep(jnp.transpose(occ_coeff, (2, 0, 1))),
        keep(jnp.transpose(vir_coeff[0], (2, 0, 1))),
    )
    return reorder(transfer_index, *got)


def solution(mesh):
    placed = (P("cell", "aux", None, None), P(), P(), P("cell", None, None, "aux"), P())
    return jax.shard_map(
        on_device,
        mesh=mesh,
        in_specs=placed,
        out_specs=P(None, "aux", None, "cell"),
        check_vma=False,
    )
```

```python
import functools

import jax
import jax.numpy as jnp
from jax import lax
from jax.experimental import pallas as pl
from jax.experimental.pallas import tpu as pltpu
from jax.sharding import PartitionSpec as P

CELLS = 64
AUX = 8
NB = 300
NO = 60
NV = 240
PIECE = NV // AUX
ROWS = 4
LANES = 128
WIDE = 2 * LANES
REST = NB - WIDE
HALF = LANES // 2
STRIPS = 5
GROUP = 16
WORKERS = 60
PAIRS = 225
SLOTS = 64
SIDE = CELLS // 2
SHARE = WORKERS // 2
FIRST, SMALL, SECOND = 0, 1, 2
MESH = pl.DeviceIdType.MESH
F32 = jnp.float32
BF16 = jnp.bfloat16


def split(x):
    high = x.astype(BF16)
    low = (x - high.astype(F32)).astype(BF16)
    return high, low


def dot(a, b, transposed=False):
    dims = (((1,), (1 if transposed else 0,)), ((), ()))
    return lax.dot_general(a, b, dims, preferred_element_type=F32)


def dot3(a, b, transposed=False):
    return (
        dot(a[0], b[0], transposed)
        + dot(a[0], b[1], transposed)
        + dot(a[1], b[0], transposed)
    )


def times_i(x, sign):
    return pltpu.roll(x, ROWS, 0) * sign


def four_points(x, sign):
    even, odd = x[0] + x[2], x[1] + x[3]
    left, right = x[0] - x[2], times_i(x[1] - x[3], sign)
    return even + odd, left + right, even - odd, left - right


def four_complex(x):
    def add(a, b):
        return a[0] + b[0], a[1] + b[1]

    def sub(a, b):
        return a[0] - b[0], a[1] - b[1]

    even, odd = add(x[0], x[2]), add(x[1], x[3])
    left, across = sub(x[0], x[2]), sub(x[1], x[3])
    return (
        add(even, odd),
        (left[0] - across[1], left[1] + across[0]),
        sub(even, odd),
        (left[0] + across[1], left[1] - across[0]),
    )


def wait_bytes(ref, sem):
    pltpu.make_async_copy(ref, ref, sem).wait()


def kernel(
    cells, blocks, occ, vir, out_0, out_1,
    cells_v, occ_v, blocks_v, pos_v, pos_s,
    sent_half_0, sent_half_1, sent_rest, got_half_0, got_half_1, got_rest,
    middle, middle_rest, whole_rest, sent_spec, sent_spec_rest, got_spec_0, got_spec_1, got_rest_0, got_rest_1,
    vir_own, vir_sent, vir_all, vir_high, vir_low, rest_high, rest_low, band, sent_pairs,
    load_sem, pos_sem, half_send, half_recv, half_local, spec_send, spec_recv, spec_local,
    pair_send, pair_recv, pair_local, vir_load_sem, vir_send, vir_recv, vir_local,
):
    me = lax.axis_index("cell")
    my_aux = lax.axis_index("aux")
    partner = my_aux + 1 - 2 * lax.rem(my_aux, 2)
    active = lax.rem(me, GROUP) != GROUP - 1
    my_slot = me - me // GROUP
    out = (out_0, out_1)
    sent_half = (sent_half_0, sent_rest, sent_half_1)
    got_half = (got_half_0, got_rest, got_half_1)
    got_spec = (got_spec_0, got_spec_1)
    got_spec_rest = (got_rest_0, got_rest_1)
    my_low, my_side = lax.rem(me, SIDE), me // SIDE

    def member(g, j):
        start = GROUP * g
        at = lax.rem(me + CELLS - start, CELLS)
        u = lax.rem(at + SIDE // 2 + (j + 1) // 2 * (1 - 2 * lax.rem(j, 2)), SIDE)
        return lax.rem(start + at // SIDE * SIDE + u, CELLS), u

    def share_slot(g):
        return lax.rem(my_slot + WORKERS - (GROUP - 1) * g, SHARE)

    def far_first(j):
        return lax.rem(me + CELLS // 2 + (j + 1) // 2 * (1 - 2 * lax.rem(j, 2)), CELLS)

    barrier = pltpu.get_barrier_semaphore()

    def greet(j, carry):
        pl.semaphore_signal(
            barrier, inc=1, device_id={"cell": far_first(j)}, device_id_type=MESH
        )
        return carry

    def greet_aux(j, carry):
        pl.semaphore_signal(
            barrier, inc=1, device_id={"aux": lax.rem(my_aux + 2 * j, AUX)}, device_id_type=MESH
        )
        return carry

    lax.fori_loop(0, CELLS - 1, greet, 0)
    lax.fori_loop(1, AUX // 2, greet_aux, 0)
    pl.semaphore_signal(barrier, inc=1, device_id={"aux": partner}, device_id_type=MESH)

    occ_loads = [pltpu.make_async_copy(occ.at[:, t, :], occ_v.at[t], load_sem.at[t]) for t in range(2)]
    block_loads = [pltpu.make_async_copy(blocks.at[:, p, :], blocks_v.at[p], load_sem.at[2 + p]) for p in range(ROWS)]
    vir_load = pltpu.make_async_copy(vir, vir_own, vir_load_sem)
    cells_load = pltpu.make_async_copy(cells, cells_v, pos_sem)
    cells_load.start()
    vir_load.start()
    for load in occ_loads + block_loads:
        load.start()
    cells_load.wait()

    folded = cells_v[...] & 3
    number = folded[0:1] * 16 + folded[1:2] * 4 + folded[2:3]
    wanted = lax.broadcasted_iota(jnp.int32, (CELLS, CELLS), 0)
    holder = lax.broadcasted_iota(jnp.int32, (CELLS, CELLS), 1)
    found = jnp.sum(jnp.where(number == wanted, holder, 0), axis=1, keepdims=True)
    pos_v[...] = jnp.broadcast_to(found & (CELLS - 1), (CELLS, LANES))
    pos_copy = pltpu.make_async_copy(pos_v, pos_s, pos_sem)
    pos_copy.start()

    def vir_slot(side, aux):
        return vir_all.at[side, :, pl.ds(aux * PIECE, PIECE)]

    def vir_copy(source, side, aux, target, sem):
        return pltpu.make_async_remote_copy(
            src_ref=source,
            dst_ref=vir_slot(side, aux),
            send_sem=vir_send.at[sem],
            recv_sem=vir_recv.at[sem],
            device_id=target,
            device_id_type=MESH,
        )

    def spread_vir(source, side):
        def one(j, carry):
            vir_copy(source, side, my_aux, {"aux": lax.rem(my_aux + 2 * j, AUX)}, 0).start()
            return carry

        lax.fori_loop(1, AUX // 2, one, 0)
        vir_copy(source, side, my_aux, {"aux": partner}, 1).start()

    vir_load.wait()
    shut = jnp.zeros((PIECE, HALF - REST), F32)
    for t in range(2):
        for n in range(2):
            vir_sent[n * 2 + t, :, 0, :] = vir_own[:, t, n * LANES : (n + 1) * LANES]
    vir_sent[STRIPS - 1, :, 0, :] = jnp.concatenate(
        [vir_own[:, 0, WIDE:NB], shut, vir_own[:, 1, WIDE:NB], shut], axis=1
    )
    pl.semaphore_wait(barrier, CELLS - 1 + AUX // 2)
    vir_copy(vir_sent, my_side, my_aux, {"cell": lax.rem(me + SIDE, CELLS)}, 2).start()
    spread_vir(vir_sent, my_side)
    own_vir = pltpu.make_async_copy(vir_sent, vir_slot(my_side, my_aux), vir_local)
    own_vir.start()

    for load in occ_loads:
        load.wait()
    blank = jnp.zeros((SLOTS - NO, NB), F32)
    left = split(jnp.concatenate([occ_v[0], blank, -occ_v[1], blank], axis=0))

    def half_product(pair):
        for load in block_loads[2 * pair : 2 * pair + 2]:
            load.wait()
        for at in range(2):
            product = dot3(left, split(blocks_v[2 * pair + at, :, 0:WIDE]))
            for t in range(2):
                for n in range(2):
                    rows = product[t * SLOTS : t * SLOTS + NO, n * LANES : (n + 1) * LANES]
                    sent_half[2 * pair][pl.ds(t * 4 + n * 2 + at, NO, stride=8), :] = rows

    def rest_product():
        gap = jnp.zeros((NB, HALF - REST), F32)
        parts = []
        for at in range(2):
            for pair in range(2):
                parts += [blocks_v[2 * pair + at, :, WIDE:NB], gap]
        product = dot3(left, split(jnp.concatenate(parts, axis=1)))
        for t in range(2):
            for at in range(2):
                sent_rest[:, t * 2 + at, :] = product[t * SLOTS : t * SLOTS + NO, at * LANES : (at + 1) * LANES]

    def half_source(part, slot):
        if part == SMALL:
            return sent_rest.at[slot]
        return sent_half[part].at[pl.ds(pl.multiple_of(slot * 8, 8), 8)]

    def send_half(part):
        def one(j, carry):
            peer = far_first(j)

            @pl.when(lax.rem(peer, GROUP) != GROUP - 1)
            def _():
                pltpu.make_async_remote_copy(
                    src_ref=half_source(part, peer - peer // GROUP),
                    dst_ref=got_half[part].at[me],
                    send_sem=half_send.at[part],
                    recv_sem=half_recv.at[part],
                    device_id={"cell": peer},
                    device_id_type=MESH,
                ).start()

            return carry

        lax.fori_loop(0, CELLS - 1, one, 0)

        @pl.when(active)
        def _():
            pltpu.make_async_copy(half_source(part, my_slot), got_half[part].at[me], half_local.at[part]).start()

    half_product(0)
    send_half(FIRST)

    half_product(1)
    rest_product()
    send_half(SMALL)
    send_half(SECOND)

    pos_copy.wait()
    first_half = lax.broadcasted_iota(jnp.int32, (2, LANES), 1) < HALF
    sign = jnp.where(lax.broadcasted_iota(jnp.int32, (8, LANES), 0) < ROWS, -1.0, 1.0).astype(F32)

    def spec_copy(part, g):
        if part == SMALL:
            return sent_spec_rest.at[g], got_spec_rest[g].at[share_slot(g)], 2 + g
        return sent_spec.at[g], got_spec[g].at[:, pl.ds(pl.multiple_of(share_slot(g) * 8, 8), 8)], g

    def arrived_half(part):
        wait_bytes(got_half[part].at[pl.ds(0, CELLS - 1)], half_recv.at[part])
        wait_bytes(got_half[part].at[0], half_local.at[part])

    def send_spec(part, g):
        sources, target, sem = spec_copy(part, g)

        def one(j, carry):
            peer, _ = member(g, j)
            pltpu.make_async_remote_copy(
                src_ref=sources.at[lax.rem(peer, SIDE)],
                dst_ref=target,
                send_sem=spec_send.at[sem],
                recv_sem=spec_recv.at[sem],
                device_id={"cell": peer},
                device_id_type=MESH,
            ).start()
            return carry

        lax.fori_loop(0, SIDE - 1, one, 0)
        pltpu.make_async_copy(sources.at[my_low], target, spec_local.at[sem]).start()

    def fourier(part):
        arrived_half(part)
        for c in range(4):
            x = [[got_half[part][pos_s[a * 16 + b * 4 + c, 0]] for b in range(4)] for a in range(4)]
            columns = [four_points([x[a][b] for a in range(4)], sign) for b in range(4)]
            for a in range(4):
                y = four_points([columns[b][a] for b in range(4)], sign)
                for b in range(4):
                    middle[a * 16 + b * 4 + c] = y[b]
        for at in range(16):
            y = four_points([middle[at * 4 + c] for c in range(4)], sign)
            for c in range(4):
                k = at * 4 + c
                sent_spec[part // 2, k % SIDE, k // SIDE] = y[c]
        send_spec(part, part // 2)

    def fourier_rest():
        arrived_half(SMALL)
        for c in range(4):
            x = [[None] * 4 for _ in range(4)]
            for a in range(4):
                for b in range(4):
                    both = got_rest[pos_s[a * 16 + b * 4 + c, 0]]
                    x[a][b] = (both[0:2], both[2:4])
            columns = [four_complex([x[a][b] for a in range(4)]) for b in range(4)]
            for a in range(4):
                y = four_complex([columns[b][a] for b in range(4)])
                for b in range(4):
                    for t in range(2):
                        middle_rest[a * 16 + b * 4 + c, 2 * t : 2 * t + 2] = y[b][t]
        for at in range(16):
            x = [(middle_rest[at * 4 + c, 0:2], middle_rest[at * 4 + c, 2:4]) for c in range(4)]
            y = four_complex(x)
            for c in range(4):
                for t in range(2):
                    whole_rest[at * 4 + c, 2 * t : 2 * t + 2] = y[c][t]
        for k in range(SIDE):
            for t in range(2):
                rows = slice(2 * t, 2 * t + 2)
                low, high = whole_rest[k, rows], whole_rest[k + SIDE, rows]
                sent_spec_rest[0, k, rows] = jnp.where(first_half, low, pltpu.roll(high, HALF, 1))
                sent_spec_rest[1, k, rows] = jnp.where(first_half, pltpu.roll(low, HALF, 1), high)
        for g in range(2):
            send_spec(SMALL, g)

    other = 1 - my_side
    wait_bytes(vir_slot(0, 0), vir_recv.at[2])
    spread_vir(vir_slot(other, my_aux), other)

    @pl.when(active)
    def _():
        fourier(FIRST)
        fourier_rest()
        fourier(SECOND)

    wait_bytes(vir_all.at[:, :, pl.ds(0, NV // 2 - PIECE)], vir_recv.at[0])

    def hand_on(j, carry):
        source = lax.rem(my_aux + 2 * j, AUX)
        for side in range(2):
            vir_copy(vir_slot(side, source), side, source, {"aux": partner}, 1).start()
        return carry

    lax.fori_loop(1, AUX // 2, hand_on, 0)
    own_vir.wait()
    wait_bytes(vir_all.at[:, :, pl.ds(0, NV // 2)], vir_recv.at[1])
    none = jnp.zeros((NV, HALF), F32)
    for side in range(2):
        rest = vir_all[side, STRIPS - 1, :, 0, :]
        for t in range(2):
            for n in range(2):
                high, low = split(vir_all[side, n * 2 + t, :, 0, :])
                at = t * WIDE + n * LANES
                vir_high[side, :, at : at + LANES] = high
                vir_low[side, :, at : at + LANES] = low
            small = rest[:, t * HALF : (t + 1) * HALF]
            high, low = split(jnp.concatenate([none, small] if side else [small, none], axis=1))
            rest_high[side, :, t * LANES : (t + 1) * LANES] = high
            rest_low[side, :, t * LANES : (t + 1) * LANES] = low

    def spec_bytes(part, g, count):
        if part == SMALL:
            return got_spec_rest[g].at[pl.ds(0, count)]
        return got_spec[g].at[:, pl.ds(0, count * 8)]

    def arrived_spec(part, g):
        sem = spec_copy(part, g)[2]

        @pl.when(active)
        def _():
            wait_bytes(spec_bytes(part, g, SHARE - 1), spec_recv.at[sem])
            wait_bytes(spec_bytes(part, g, 1), spec_local.at[sem])

        @pl.when(jnp.logical_not(active))
        def _():
            wait_bytes(spec_bytes(part, g, SHARE), spec_recv.at[sem])

    def turned(even, odd):
        upper = jnp.concatenate(even + [-x for x in odd], axis=1)
        lower = jnp.concatenate(odd + even, axis=1)
        return [upper, lower]

    lane = lax.broadcasted_iota(jnp.int32, (ROWS, WIDE), 1)

    def band_and_pairs(g):
        arrived_spec(2 * g, g)
        arrived_spec(SMALL, g)
        for side in range(2):
            main, small = [], []
            for at in range(2):
                x = [
                    [got_spec[g][side, pl.ds(t * 4 + n * 2 + at, SIDE, stride=8), :] for n in range(2)]
                    for t in range(2)
                ]
                main += turned(x[0], x[1])
                y = [got_spec_rest[g][:, t * 2 + at, :] for t in range(2)]
                small += turned([y[0]], [y[1]])
            value = dot3(split(jnp.concatenate(main, axis=0)), (vir_high[side], vir_low[side]), transposed=True)
            value = value + dot3(split(jnp.concatenate(small, axis=0)), (rest_high[side], rest_low[side]), transposed=True)
            value = jnp.concatenate([value, jnp.zeros((4 * SIDE, WIDE - NV), F32)], axis=1)
            for at in range(2):
                for t in range(2):
                    start = (at * 2 + t) * SIDE
                    for n in range(2):
                        band[g, side, n, pl.ds(t * 2 + at, SHARE, stride=4), :] = value[
                            start : start + SHARE, n * LANES : (n + 1) * LANES
                        ]

        for block in range(2):
            base = block * (GROUP - 1)
            for side in range(2):

                def wide(i):
                    return jnp.concatenate([band[g, side, n, 4 * i : 4 * i + 4, :] for n in range(2)], axis=1)

                for m in range(GROUP):
                    shift = (NV - PAIRS) * m
                    if m == 0:
                        chunk = wide(base)
                    else:
                        chunk = pltpu.roll(wide(base + m - 1), WIDE - (NV - shift), 1)
                        if m < GROUP - 1:
                            chunk = jnp.where(lane < shift, chunk, pltpu.roll(wide(base + m), shift, 1))
                    sent_pairs[g, block * GROUP + m, side] = chunk

        def one(j, carry):
            peer, u = member(g, j)
            pltpu.make_async_remote_copy(
                src_ref=sent_pairs.at[g, u],
                dst_ref=out[g].at[my_low],
                send_sem=pair_send.at[g],
                recv_sem=pair_recv.at[g],
                device_id={"cell": peer},
                device_id_type=MESH,
            ).start()
            return carry

        lax.fori_loop(0, SIDE - 1, one, 0)
        my_place = lax.rem(me + CELLS - GROUP * g, SIDE)
        pltpu.make_async_copy(sent_pairs.at[g, my_place], out[g].at[my_low], pair_local.at[g]).start()

    for g in range(2):
        band_and_pairs(g)

    for part in (FIRST, SMALL, SECOND):
        step = 1 if part == SMALL else 8

        @pl.when(active)
        def _():
            wait_bytes(sent_half[part].at[pl.ds(0, (WORKERS - 1) * step)], half_send.at[part])

        @pl.when(jnp.logical_not(active))
        def _():
            wait_bytes(sent_half[part].at[pl.ds(0, WORKERS * step)], half_send.at[part])

    @pl.when(active)
    def _():
        for g in range(2):
            wait_bytes(sent_spec.at[g, pl.ds(0, SIDE - 1)], spec_send.at[g])
            wait_bytes(sent_spec_rest.at[g, pl.ds(0, SIDE - 1)], spec_send.at[2 + g])

    wait_bytes(vir_all.at[:, :, pl.ds(0, NV // 2 - PIECE)], vir_send.at[0])
    wait_bytes(vir_all.at[:, :, pl.ds(0, NV // 2)], vir_send.at[1])
    wait_bytes(vir_slot(0, 0), vir_send.at[2])
    for g in range(2):
        wait_bytes(sent_pairs.at[g, pl.ds(0, SIDE - 1)], pair_send.at[g])
        wait_bytes(out[g].at[0], pair_local.at[g])
        wait_bytes(out[g].at[pl.ds(0, SIDE - 1)], pair_recv.at[g])


def exchange(cells, blocks, occ, vir):
    dma = pltpu.SemaphoreType.DMA
    pairs = jax.ShapeDtypeStruct((SIDE, 2, ROWS, WIDE), F32)
    tiles = pltpu.VMEM((CELLS, 8, LANES), F32)
    halves = pltpu.VMEM((SLOTS, 4, LANES), F32)
    return pl.pallas_call(
        kernel,
        out_shape=(pairs, pairs),
        in_specs=[
            pl.BlockSpec(memory_space=pl.ANY),
            pl.BlockSpec(memory_space=pl.ANY),
            pl.BlockSpec(memory_space=pl.ANY),
            pl.BlockSpec(memory_space=pl.ANY),
        ],
        out_specs=(pl.BlockSpec(memory_space=pltpu.VMEM), pl.BlockSpec(memory_space=pltpu.VMEM)),
        scratch_shapes=[
            pltpu.VMEM((3, CELLS), jnp.int32),
            pltpu.VMEM((2, NO, NB), F32),
            pltpu.VMEM((ROWS, NB, NB), F32),
            pltpu.VMEM((CELLS, LANES), jnp.int32),
            pltpu.SMEM((CELLS, LANES), jnp.int32),
            pltpu.VMEM((WORKERS * 8, LANES), F32),
            pltpu.VMEM((WORKERS * 8, LANES), F32),
            pltpu.VMEM((WORKERS, 4, LANES), F32),
            tiles,
            tiles,
            halves,
            tiles,
            halves,
            halves,
            pltpu.VMEM((2, SIDE, 2, 8, LANES), F32),
            pltpu.VMEM((2, SIDE, 4, LANES), F32),
            pltpu.VMEM((2, SIDE * 8, LANES), F32),
            pltpu.VMEM((2, SIDE * 8, LANES), F32),
            pltpu.VMEM((SIDE, 4, LANES), F32),
            pltpu.VMEM((SIDE, 4, LANES), F32),
            pltpu.VMEM((PIECE, 2, NB), F32),
            pltpu.VMEM((STRIPS, PIECE, 1, LANES), F32),
            pltpu.VMEM((2, STRIPS, NV, 1, LANES), F32),
            pltpu.VMEM((2, NV, 2 * WIDE), BF16),
            pltpu.VMEM((2, NV, 2 * WIDE), BF16),
            pltpu.VMEM((2, NV, WIDE), BF16),
            pltpu.VMEM((2, NV, WIDE), BF16),
            pltpu.VMEM((2, 2, 2, SHARE * 4, LANES), F32),
            pltpu.VMEM((2, SIDE, 2, ROWS, WIDE), F32),
            dma((2 + ROWS,)),
            dma,
            dma((3,)),
            dma((3,)),
            dma((3,)),
            dma((4,)),
            dma((4,)),
            dma((4,)),
            dma((2,)),
            dma((2,)),
            dma((2,)),
            dma,
            dma((3,)),
            dma((3,)),
            dma,
        ],
        compiler_params=pltpu.CompilerParams(
            collective_id=0, has_side_effects=True, vmem_limit_bytes=44 << 20
        ),
        name="transform",
    )(cells, blocks, occ, vir)


def reorder_kernel(transfer, got_0, got_1, out, rows, ordered, sem):
    first = transfer[0]
    shifts = (first // 16, first // 4 % 4, first % 4)
    along = [[(n - shift) & 3 for n in range(4)] for shift in shifts]
    copies = []
    for g, got in enumerate((got_0, got_1)):
        for q in range(CELLS):
            source = along[0][q // 16] * 16 + along[1][q // 4 % 4] * 4 + along[2][q % 4]
            tile = got[source & (SIDE - 1), source >> 5]
            for t in range(2):
                for n in range(2):
                    at = (t * ROWS + 2 * g) * CELLS + q
                    rows[n, pl.ds(at, 2, stride=CELLS), :] = tile[2 * t : 2 * t + 2, n * LANES : (n + 1) * LANES]
        for t in range(2):
            for p in (2 * g, 2 * g + 1):
                at = (t * ROWS + p) * CELLS
                ordered[t, p, :, 0:LANES] = rows[0, at : at + CELLS, :]
                ordered[t, p, :, LANES:PAIRS] = rows[1, at : at + CELLS, 0 : PAIRS - LANES]
            both = pl.ds(2 * g, 2)
            copy = pltpu.make_async_copy(ordered.at[t, both], out.at[t, both], sem.at[g, t])
            copy.start()
            copies.append(copy)
    for copy in copies:
        copy.wait()


def reorder(transfer, got_0, got_1):
    whole = pl.BlockSpec(memory_space=pltpu.VMEM)
    return pl.pallas_call(
        reorder_kernel,
        out_shape=jax.ShapeDtypeStruct((2, ROWS, CELLS, PAIRS), F32),
        in_specs=[pl.BlockSpec(memory_space=pltpu.SMEM), whole, whole],
        out_specs=pl.BlockSpec(memory_space=pl.ANY),
        scratch_shapes=[
            pltpu.VMEM((2, 2 * ROWS * CELLS, LANES), F32),
            pltpu.VMEM((2, ROWS, CELLS, PAIRS), F32),
            pltpu.SemaphoreType.DMA((2, 2)),
        ],
        compiler_params=pltpu.CompilerParams(vmem_limit_bytes=16 << 20),
        name="reorder",
    )(transfer, got_0, got_1)


def on_device(blocks, cell_offsets, occ_coeff, vir_coeff, transfer_index):
    keep = functools.partial(pltpu.with_memory_space_constraint, memory_space=pltpu.HBM)
    got = exchange(
        keep(cell_offsets),
        keep(jnp.transpose(blocks[0], (1, 0, 2))),
        keep(jnp.transpose(occ_coeff, (2, 0, 1))),
        keep(jnp.transpose(vir_coeff[0], (2, 0, 1))),
    )
    return reorder(transfer_index, *got)


def solution(mesh):
    placed = (P("cell", "aux", None, None), P(), P(), P("cell", None, None, "aux"), P())
    return jax.shard_map(
        on_device,
        mesh=mesh,
        in_specs=placed,
        out_specs=P(None, "aux", None, "cell"),
        check_vma=False,
    )
```

```python
import functools

import jax
import jax.numpy as jnp
from jax import lax
from jax.experimental import pallas as pl
from jax.experimental.pallas import tpu as pltpu
from jax.sharding import PartitionSpec as P

CELLS = 64
AUX = 8
NB = 300
NO = 60
NV = 240
PIECE = NV // AUX
ROWS = 4
LANES = 128
WIDE = 2 * LANES
REST = NB - WIDE
HALF = LANES // 2
STRIPS = 5
GROUP = 16
WORKERS = 60
PAIRS = 225
SLOTS = 64
SIDE = CELLS // 2
SHARE = WORKERS // 2
FIRST, SMALL, SECOND = 0, 1, 2
MESH = pl.DeviceIdType.MESH
F32 = jnp.float32
BF16 = jnp.bfloat16


def split(x):
    high = x.astype(BF16)
    low = (x - high.astype(F32)).astype(BF16)
    return high, low


def dot(a, b, transposed=False):
    dims = (((1,), (1 if transposed else 0,)), ((), ()))
    return lax.dot_general(a, b, dims, preferred_element_type=F32)


def dot3(a, b, transposed=False):
    return (
        dot(a[0], b[0], transposed)
        + dot(a[0], b[1], transposed)
        + dot(a[1], b[0], transposed)
    )


def times_i(x, sign):
    return pltpu.roll(x, ROWS, 0) * sign


def four_points(x, sign):
    even, odd = x[0] + x[2], x[1] + x[3]
    left, right = x[0] - x[2], times_i(x[1] - x[3], sign)
    return even + odd, left + right, even - odd, left - right


def four_complex(x):
    def add(a, b):
        return a[0] + b[0], a[1] + b[1]

    def sub(a, b):
        return a[0] - b[0], a[1] - b[1]

    even, odd = add(x[0], x[2]), add(x[1], x[3])
    left, across = sub(x[0], x[2]), sub(x[1], x[3])
    return (
        add(even, odd),
        (left[0] - across[1], left[1] + across[0]),
        sub(even, odd),
        (left[0] + across[1], left[1] - across[0]),
    )


def wrapped(x, length):
    return jnp.where(x >= length, x - length, x)


def wait_bytes(ref, sem):
    pltpu.make_async_copy(ref, ref, sem).wait()


def kernel(
    cells, blocks, occ, vir, out_0, out_1,
    cells_v, occ_v, blocks_v, pos_v, pos_s,
    sent_half_0, sent_half_1, sent_rest, got_half_0, got_half_1, got_rest,
    middle, middle_rest, whole_rest, sent_spec, sent_spec_rest, got_spec_0, got_spec_1, got_rest_0, got_rest_1,
    vir_own, vir_sent, vir_all, vir_high, vir_low, rest_high, rest_low, band, sent_pairs,
    load_sem, pos_sem, half_send, half_recv, half_local, spec_send, spec_recv, spec_local,
    pair_send, pair_recv, pair_local, vir_load_sem, vir_send, vir_recv, vir_local,
):
    me = lax.axis_index("cell")
    my_aux = lax.axis_index("aux")
    partner = my_aux + 1 - 2 * lax.rem(my_aux, 2)
    active = lax.rem(me, GROUP) != GROUP - 1
    my_slot = me - me // GROUP
    out = (out_0, out_1)
    sent_half = (sent_half_0, sent_rest, sent_half_1)
    got_half = (got_half_0, got_rest, got_half_1)
    got_spec = (got_spec_0, got_spec_1)
    got_spec_rest = (got_rest_0, got_rest_1)
    my_low, my_side = lax.rem(me, SIDE), me // SIDE
    my_block = me // GROUP
    my_first = wrapped(lax.rem(me, GROUP), GROUP - 1)
    share_at, share_start = [], []
    for g in range(2):
        place = wrapped(me + CELLS - GROUP * g, CELLS)
        share_at.append(lax.rem(place, SIDE))
        share_start.append(GROUP * g + place // SIDE * SIDE)

    def for_members(g, send):
        def at(offset):
            u = wrapped(share_at[g] + offset, SIDE)
            send(wrapped(share_start[g] + u, CELLS), u)

        def one(j, carry):
            at(SIDE // 2 - j)
            at(SIDE // 2 + j)
            return carry

        at(SIDE // 2)
        lax.fori_loop(1, SIDE // 2, one, 0)

    def share_slot(g):
        return lax.rem(my_slot + WORKERS - (GROUP - 1) * g, SHARE)

    occ_loads = [pltpu.make_async_copy(occ.at[:, t, :], occ_v.at[t], load_sem.at[t]) for t in range(2)]
    block_loads = [pltpu.make_async_copy(blocks.at[:, p, :], blocks_v.at[p], load_sem.at[2 + p]) for p in range(ROWS)]
    vir_load = pltpu.make_async_copy(vir, vir_own, vir_load_sem)
    cells_load = pltpu.make_async_copy(cells, cells_v, pos_sem)
    cells_load.start()
    vir_load.start()
    for load in occ_loads + block_loads:
        load.start()


    barrier = pltpu.get_barrier_semaphore()

    def greet(j, carry):
        for offset in (SIDE - j, SIDE + j):
            pl.semaphore_signal(
                barrier, inc=1, device_id={"cell": wrapped(me + offset, CELLS)}, device_id_type=MESH
            )
        return carry

    def greet_aux(j, carry):
        pl.semaphore_signal(
            barrier, inc=1, device_id={"aux": lax.rem(my_aux + 2 * j, AUX)}, device_id_type=MESH
        )
        return carry

    pl.semaphore_signal(barrier, inc=1, device_id={"cell": wrapped(me + SIDE, CELLS)}, device_id_type=MESH)
    lax.fori_loop(1, SIDE, greet, 0)
    lax.fori_loop(1, AUX // 2, greet_aux, 0)
    pl.semaphore_signal(barrier, inc=1, device_id={"aux": partner}, device_id_type=MESH)

    cells_load.wait()
    folded = cells_v[...] & 3
    number = folded[0:1] * 16 + folded[1:2] * 4 + folded[2:3]
    wanted = lax.broadcasted_iota(jnp.int32, (CELLS, CELLS), 0)
    holder = lax.broadcasted_iota(jnp.int32, (CELLS, CELLS), 1)
    found = jnp.sum(jnp.where(number == wanted, holder, 0), axis=1, keepdims=True)
    pos_v[...] = jnp.broadcast_to(found & (CELLS - 1), (CELLS, LANES))
    pos_copy = pltpu.make_async_copy(pos_v, pos_s, pos_sem)
    pos_copy.start()

    def vir_slot(side, aux):
        return vir_all.at[side, :, pl.ds(aux * PIECE, PIECE)]

    def vir_copy(source, side, aux, target, sem):
        return pltpu.make_async_remote_copy(
            src_ref=source,
            dst_ref=vir_slot(side, aux),
            send_sem=vir_send.at[sem],
            recv_sem=vir_recv.at[sem],
            device_id=target,
            device_id_type=MESH,
        )

    def spread_vir(source, side):
        def one(j, carry):
            vir_copy(source, side, my_aux, {"aux": lax.rem(my_aux + 2 * j, AUX)}, 0).start()
            return carry

        lax.fori_loop(1, AUX // 2, one, 0)
        vir_copy(source, side, my_aux, {"aux": partner}, 1).start()

    vir_load.wait()
    shut = jnp.zeros((PIECE, HALF - REST), F32)
    for t in range(2):
        for n in range(2):
            vir_sent[n * 2 + t, :, 0, :] = vir_own[:, t, n * LANES : (n + 1) * LANES]
    vir_sent[STRIPS - 1, :, 0, :] = jnp.concatenate(
        [vir_own[:, 0, WIDE:NB], shut, vir_own[:, 1, WIDE:NB], shut], axis=1
    )
    pl.semaphore_wait(barrier, CELLS - 1 + AUX // 2)
    vir_copy(vir_sent, my_side, my_aux, {"cell": lax.rem(me + SIDE, CELLS)}, 2).start()
    spread_vir(vir_sent, my_side)
    own_vir = pltpu.make_async_copy(vir_sent, vir_slot(my_side, my_aux), vir_local)
    own_vir.start()

    for load in occ_loads:
        load.wait()
    blank = jnp.zeros((SLOTS - NO, NB), F32)
    left = split(jnp.concatenate([occ_v[0], blank, -occ_v[1], blank], axis=0))

    def half_product(pair):
        for load in block_loads[2 * pair : 2 * pair + 2]:
            load.wait()
        for at in range(2):
            product = dot3(left, split(blocks_v[2 * pair + at, :, 0:WIDE]))
            for t in range(2):
                for n in range(2):
                    rows = product[t * SLOTS : t * SLOTS + NO, n * LANES : (n + 1) * LANES]
                    sent_half[2 * pair][pl.ds(t * 4 + n * 2 + at, NO, stride=8), :] = rows

    def rest_product():
        gap = jnp.zeros((NB, HALF - REST), F32)
        parts = []
        for at in range(2):
            for pair in range(2):
                parts += [blocks_v[2 * pair + at, :, WIDE:NB], gap]
        product = dot3(left, split(jnp.concatenate(parts, axis=1)))
        for t in range(2):
            for at in range(2):
                sent_rest[:, t * 2 + at, :] = product[t * SLOTS : t * SLOTS + NO, at * LANES : (at + 1) * LANES]

    def half_source(part, slot):
        if part == SMALL:
            return sent_rest.at[slot]
        return sent_half[part].at[pl.ds(pl.multiple_of(slot * 8, 8), 8)]

    def send_half(part):
        for turn in (2, 3, 1, 0):
            block = wrapped(my_block + turn, 4)

            def one(j, carry):
                m = wrapped(j + my_first, GROUP - 1)
                peer = block * GROUP + m

                def send():
                    pltpu.make_async_remote_copy(
                        src_ref=half_source(part, block * (GROUP - 1) + m),
                        dst_ref=got_half[part].at[me],
                        send_sem=half_send.at[part],
                        recv_sem=half_recv.at[part],
                        device_id={"cell": peer},
                        device_id_type=MESH,
                    ).start()

                if turn:
                    send()
                else:
                    pl.when(peer != me)(send)
                return carry

            lax.fori_loop(0, GROUP - 1, one, 0)

        @pl.when(active)
        def _():
            pltpu.make_async_copy(half_source(part, my_slot), got_half[part].at[me], half_local.at[part]).start()

    half_product(0)
    send_half(FIRST)

    half_product(1)
    rest_product()
    send_half(SMALL)
    send_half(SECOND)

    pos_copy.wait()
    first_half = lax.broadcasted_iota(jnp.int32, (2, LANES), 1) < HALF
    sign = jnp.where(lax.broadcasted_iota(jnp.int32, (8, LANES), 0) < ROWS, -1.0, 1.0).astype(F32)

    def spec_copy(part, g):
        if part == SMALL:
            return sent_spec_rest.at[g], got_spec_rest[g].at[share_slot(g)], 2 + g
        return sent_spec.at[g], got_spec[g].at[:, pl.ds(pl.multiple_of(share_slot(g) * 8, 8), 8)], g

    def arrived_half(part):
        wait_bytes(got_half[part].at[pl.ds(0, CELLS - 1)], half_recv.at[part])
        wait_bytes(got_half[part].at[0], half_local.at[part])

    def send_spec(part, g):
        sources, target, sem = spec_copy(part, g)

        def send(peer, u):
            pltpu.make_async_remote_copy(
                src_ref=sources.at[wrapped(peer, SIDE)],
                dst_ref=target,
                send_sem=spec_send.at[sem],
                recv_sem=spec_recv.at[sem],
                device_id={"cell": peer},
                device_id_type=MESH,
            ).start()

        for_members(g, send)
        pltpu.make_async_copy(sources.at[my_low], target, spec_local.at[sem]).start()

    def fourier(part):
        arrived_half(part)
        for c in range(4):
            x = [[got_half[part][pos_s[a * 16 + b * 4 + c, 0]] for b in range(4)] for a in range(4)]
            columns = [four_points([x[a][b] for a in range(4)], sign) for b in range(4)]
            for a in range(4):
                y = four_points([columns[b][a] for b in range(4)], sign)
                for b in range(4):
                    middle[a * 16 + b * 4 + c] = y[b]
        for at in range(16):
            y = four_points([middle[at * 4 + c] for c in range(4)], sign)
            for c in range(4):
                k = at * 4 + c
                sent_spec[part // 2, k % SIDE, k // SIDE] = y[c]
        send_spec(part, part // 2)

    def fourier_rest():
        arrived_half(SMALL)
        for c in range(4):
            x = [[None] * 4 for _ in range(4)]
            for a in range(4):
                for b in range(4):
                    both = got_rest[pos_s[a * 16 + b * 4 + c, 0]]
                    x[a][b] = (both[0:2], both[2:4])
            columns = [four_complex([x[a][b] for a in range(4)]) for b in range(4)]
            for a in range(4):
                y = four_complex([columns[b][a] for b in range(4)])
                for b in range(4):
                    for t in range(2):
                        middle_rest[a * 16 + b * 4 + c, 2 * t : 2 * t + 2] = y[b][t]
        for at in range(16):
            x = [(middle_rest[at * 4 + c, 0:2], middle_rest[at * 4 + c, 2:4]) for c in range(4)]
            y = four_complex(x)
            for c in range(4):
                for t in range(2):
                    whole_rest[at * 4 + c, 2 * t : 2 * t + 2] = y[c][t]
        for k in range(SIDE):
            for t in range(2):
                rows = slice(2 * t, 2 * t + 2)
                low, high = whole_rest[k, rows], whole_rest[k + SIDE, rows]
                sent_spec_rest[0, k, rows] = jnp.where(first_half, low, pltpu.roll(high, HALF, 1))
                sent_spec_rest[1, k, rows] = jnp.where(first_half, pltpu.roll(low, HALF, 1), high)
        for g in range(2):
            send_spec(SMALL, g)

    other = 1 - my_side
    wait_bytes(vir_slot(0, 0), vir_recv.at[2])
    spread_vir(vir_slot(other, my_aux), other)

    @pl.when(active)
    def _():
        fourier(FIRST)
        fourier_rest()
        fourier(SECOND)

    wait_bytes(vir_all.at[:, :, pl.ds(0, NV // 2 - PIECE)], vir_recv.at[0])

    def hand_on(j, carry):
        source = lax.rem(my_aux + 2 * j, AUX)
        for side in range(2):
            vir_copy(vir_slot(side, source), side, source, {"aux": partner}, 1).start()
        return carry

    lax.fori_loop(1, AUX // 2, hand_on, 0)
    own_vir.wait()
    wait_bytes(vir_all.at[:, :, pl.ds(0, NV // 2)], vir_recv.at[1])
    none = jnp.zeros((NV, HALF), F32)
    for side in range(2):
        rest = vir_all[side, STRIPS - 1, :, 0, :]
        for t in range(2):
            for n in range(2):
                high, low = split(vir_all[side, n * 2 + t, :, 0, :])
                at = t * WIDE + n * LANES
                vir_high[side, :, at : at + LANES] = high
                vir_low[side, :, at : at + LANES] = low
            small = rest[:, t * HALF : (t + 1) * HALF]
            high, low = split(jnp.concatenate([none, small] if side else [small, none], axis=1))
            rest_high[side, :, t * LANES : (t + 1) * LANES] = high
            rest_low[side, :, t * LANES : (t + 1) * LANES] = low

    def spec_bytes(part, g, count):
        if part == SMALL:
            return got_spec_rest[g].at[pl.ds(0, count)]
        return got_spec[g].at[:, pl.ds(0, count * 8)]

    def arrived_spec(part, g):
        sem = spec_copy(part, g)[2]

        @pl.when(active)
        def _():
            wait_bytes(spec_bytes(part, g, SHARE - 1), spec_recv.at[sem])
            wait_bytes(spec_bytes(part, g, 1), spec_local.at[sem])

        @pl.when(jnp.logical_not(active))
        def _():
            wait_bytes(spec_bytes(part, g, SHARE), spec_recv.at[sem])

    def turned(even, odd):
        upper = jnp.concatenate(even + [-x for x in odd], axis=1)
        lower = jnp.concatenate(odd + even, axis=1)
        return [upper, lower]

    lane = lax.broadcasted_iota(jnp.int32, (ROWS, WIDE), 1)

    def band_and_pairs(g):
        arrived_spec(2 * g, g)
        arrived_spec(SMALL, g)
        for side in range(2):
            main, small = [], []
            for at in range(2):
                x = [
                    [got_spec[g][side, pl.ds(t * 4 + n * 2 + at, SIDE, stride=8), :] for n in range(2)]
                    for t in range(2)
                ]
                main += turned(x[0], x[1])
                y = [got_spec_rest[g][:, t * 2 + at, :] for t in range(2)]
                small += turned([y[0]], [y[1]])
            value = dot3(split(jnp.concatenate(main, axis=0)), (vir_high[side], vir_low[side]), transposed=True)
            value = value + dot3(split(jnp.concatenate(small, axis=0)), (rest_high[side], rest_low[side]), transposed=True)
            value = jnp.concatenate([value, jnp.zeros((4 * SIDE, WIDE - NV), F32)], axis=1)
            for at in range(2):
                for t in range(2):
                    start = (at * 2 + t) * SIDE
                    for n in range(2):
                        band[g, side, n, pl.ds(t * 2 + at, SHARE, stride=4), :] = value[
                            start : start + SHARE, n * LANES : (n + 1) * LANES
                        ]

        for block in range(2):
            base = block * (GROUP - 1)
            for side in range(2):

                def wide(i):
                    return jnp.concatenate([band[g, side, n, 4 * i : 4 * i + 4, :] for n in range(2)], axis=1)

                for m in range(GROUP):
                    shift = (NV - PAIRS) * m
                    if m == 0:
                        chunk = wide(base)
                    else:
                        chunk = pltpu.roll(wide(base + m - 1), WIDE - (NV - shift), 1)
                        if m < GROUP - 1:
                            chunk = jnp.where(lane < shift, chunk, pltpu.roll(wide(base + m), shift, 1))
                    sent_pairs[g, block * GROUP + m, side] = chunk

        def send(peer, u):
            pltpu.make_async_remote_copy(
                src_ref=sent_pairs.at[g, u],
                dst_ref=out[g].at[my_low],
                send_sem=pair_send.at[g],
                recv_sem=pair_recv.at[g],
                device_id={"cell": peer},
                device_id_type=MESH,
            ).start()

        for_members(g, send)
        pltpu.make_async_copy(sent_pairs.at[g, share_at[g]], out[g].at[my_low], pair_local.at[g]).start()

    for g in range(2):
        band_and_pairs(g)

    for part in (FIRST, SMALL, SECOND):
        step = 1 if part == SMALL else 8

        @pl.when(active)
        def _():
            wait_bytes(sent_half[part].at[pl.ds(0, (WORKERS - 1) * step)], half_send.at[part])

        @pl.when(jnp.logical_not(active))
        def _():
            wait_bytes(sent_half[part].at[pl.ds(0, WORKERS * step)], half_send.at[part])

    @pl.when(active)
    def _():
        for g in range(2):
            wait_bytes(sent_spec.at[g, pl.ds(0, SIDE - 1)], spec_send.at[g])
            wait_bytes(sent_spec_rest.at[g, pl.ds(0, SIDE - 1)], spec_send.at[2 + g])

    wait_bytes(vir_all.at[:, :, pl.ds(0, NV // 2 - PIECE)], vir_send.at[0])
    wait_bytes(vir_all.at[:, :, pl.ds(0, NV // 2)], vir_send.at[1])
    wait_bytes(vir_slot(0, 0), vir_send.at[2])
    for g in range(2):
        wait_bytes(sent_pairs.at[g, pl.ds(0, SIDE - 1)], pair_send.at[g])
        wait_bytes(out[g].at[0], pair_local.at[g])
        wait_bytes(out[g].at[pl.ds(0, SIDE - 1)], pair_recv.at[g])


def exchange(cells, blocks, occ, vir):
    dma = pltpu.SemaphoreType.DMA
    pairs = jax.ShapeDtypeStruct((SIDE, 2, ROWS, WIDE), F32)
    tiles = pltpu.VMEM((CELLS, 8, LANES), F32)
    halves = pltpu.VMEM((SLOTS, 4, LANES), F32)
    return pl.pallas_call(
        kernel,
        out_shape=(pairs, pairs),
        in_specs=[
            pl.BlockSpec(memory_space=pl.ANY),
            pl.BlockSpec(memory_space=pl.ANY),
            pl.BlockSpec(memory_space=pl.ANY),
            pl.BlockSpec(memory_space=pl.ANY),
        ],
        out_specs=(pl.BlockSpec(memory_space=pltpu.VMEM), pl.BlockSpec(memory_space=pltpu.VMEM)),
        scratch_shapes=[
            pltpu.VMEM((3, CELLS), jnp.int32),
            pltpu.VMEM((2, NO, NB), F32),
            pltpu.VMEM((ROWS, NB, NB), F32),
            pltpu.VMEM((CELLS, LANES), jnp.int32),
            pltpu.SMEM((CELLS, LANES), jnp.int32),
            pltpu.VMEM((WORKERS * 8, LANES), F32),
            pltpu.VMEM((WORKERS * 8, LANES), F32),
            pltpu.VMEM((WORKERS, 4, LANES), F32),
            tiles,
            tiles,
            halves,
            tiles,
            halves,
            halves,
            pltpu.VMEM((2, SIDE, 2, 8, LANES), F32),
            pltpu.VMEM((2, SIDE, 4, LANES), F32),
            pltpu.VMEM((2, SIDE * 8, LANES), F32),
            pltpu.VMEM((2, SIDE * 8, LANES), F32),
            pltpu.VMEM((SIDE, 4, LANES), F32),
            pltpu.VMEM((SIDE, 4, LANES), F32),
            pltpu.VMEM((PIECE, 2, NB), F32),
            pltpu.VMEM((STRIPS, PIECE, 1, LANES), F32),
            pltpu.VMEM((2, STRIPS, NV, 1, LANES), F32),
            pltpu.VMEM((2, NV, 2 * WIDE), BF16),
            pltpu.VMEM((2, NV, 2 * WIDE), BF16),
            pltpu.VMEM((2, NV, WIDE), BF16),
            pltpu.VMEM((2, NV, WIDE), BF16),
            pltpu.VMEM((2, 2, 2, SHARE * 4, LANES), F32),
            pltpu.VMEM((2, SIDE, 2, ROWS, WIDE), F32),
            dma((2 + ROWS,)),
            dma,
            dma((3,)),
            dma((3,)),
            dma((3,)),
            dma((4,)),
            dma((4,)),
            dma((4,)),
            dma((2,)),
            dma((2,)),
            dma((2,)),
            dma,
            dma((3,)),
            dma((3,)),
            dma,
        ],
        compiler_params=pltpu.CompilerParams(
            collective_id=0, has_side_effects=True, vmem_limit_bytes=44 << 20
        ),
        name="transform",
    )(cells, blocks, occ, vir)


def reorder_kernel(transfer, got_0, got_1, out, rows, ordered, sem):
    first = transfer[0]
    shifts = (first // 16, first // 4 % 4, first % 4)
    along = [[(n - shift) & 3 for n in range(4)] for shift in shifts]
    copies = []
    for g, got in enumerate((got_0, got_1)):
        for q in range(CELLS):
            source = along[0][q // 16] * 16 + along[1][q // 4 % 4] * 4 + along[2][q % 4]
            tile = got[source & (SIDE - 1), source >> 5]
            for t in range(2):
                for n in range(2):
                    at = (t * ROWS + 2 * g) * CELLS + q
                    rows[n, pl.ds(at, 2, stride=CELLS), :] = tile[2 * t : 2 * t + 2, n * LANES : (n + 1) * LANES]
        for t in range(2):
            for p in (2 * g, 2 * g + 1):
                at = (t * ROWS + p) * CELLS
                ordered[t, p, :, 0:LANES] = rows[0, at : at + CELLS, :]
                ordered[t, p, :, LANES:PAIRS] = rows[1, at : at + CELLS, 0 : PAIRS - LANES]
            both = pl.ds(2 * g, 2)
            copy = pltpu.make_async_copy(ordered.at[t, both], out.at[t, both], sem.at[g, t])
            copy.start()
            copies.append(copy)
    for copy in copies:
        copy.wait()


def reorder(transfer, got_0, got_1):
    whole = pl.BlockSpec(memory_space=pltpu.VMEM)
    return pl.pallas_call(
        reorder_kernel,
        out_shape=jax.ShapeDtypeStruct((2, ROWS, CELLS, PAIRS), F32),
        in_specs=[pl.BlockSpec(memory_space=pltpu.SMEM), whole, whole],
        out_specs=pl.BlockSpec(memory_space=pl.ANY),
        scratch_shapes=[
            pltpu.VMEM((2, 2 * ROWS * CELLS, LANES), F32),
            pltpu.VMEM((2, ROWS, CELLS, PAIRS), F32),
            pltpu.SemaphoreType.DMA((2, 2)),
        ],
        compiler_params=pltpu.CompilerParams(vmem_limit_bytes=16 << 20),
        name="reorder",
    )(transfer, got_0, got_1)


def on_device(blocks, cell_offsets, occ_coeff, vir_coeff, transfer_index):
    keep = functools.partial(pltpu.with_memory_space_constraint, memory_space=pltpu.HBM)
    got = exchange(
        keep(cell_offsets),
        keep(jnp.transpose(blocks[0], (1, 0, 2))),
        keep(jnp.transpose(occ_coeff, (2, 0, 1))),
        keep(jnp.transpose(vir_coeff[0], (2, 0, 1))),
    )
    return reorder(transfer_index, *got)


def solution(mesh):
    placed = (P("cell", "aux", None, None), P(), P(), P("cell", None, None, "aux"), P())
    return jax.shard_map(
        on_device,
        mesh=mesh,
        in_specs=placed,
        out_specs=P(None, "aux", None, "cell"),
        check_vma=False,
    )
```

```python
import functools

import jax
import jax.numpy as jnp
from jax import lax
from jax.experimental import pallas as pl
from jax.experimental.pallas import tpu as pltpu
from jax.sharding import PartitionSpec as P

CELLS = 64
AUX = 8
NB = 300
NO = 60
NV = 240
PIECE = NV // AUX
ROWS = 4
LANES = 128
WIDE = 2 * LANES
REST = NB - WIDE
HALF = LANES // 2
STRIPS = 5
GROUP = 16
WORKERS = 60
PAIRS = 225
SLOTS = 64
SIDE = CELLS // 2
SHARE = WORKERS // 2
FIRST, SMALL, SECOND = 0, 1, 2
MESH = pl.DeviceIdType.MESH
F32 = jnp.float32
BF16 = jnp.bfloat16


def split(x):
    high = x.astype(BF16)
    low = (x - high.astype(F32)).astype(BF16)
    return high, low


def dot(a, b, transposed=False):
    dims = (((1,), (1 if transposed else 0,)), ((), ()))
    return lax.dot_general(a, b, dims, preferred_element_type=F32)


def dot3(a, b, transposed=False):
    return (
        dot(a[0], b[0], transposed)
        + dot(a[0], b[1], transposed)
        + dot(a[1], b[0], transposed)
    )


def times_i(x, sign):
    return pltpu.roll(x, ROWS, 0) * sign


def four_points(x, sign):
    even, odd = x[0] + x[2], x[1] + x[3]
    left, right = x[0] - x[2], times_i(x[1] - x[3], sign)
    return even + odd, left + right, even - odd, left - right


def four_complex(x):
    def add(a, b):
        return a[0] + b[0], a[1] + b[1]

    def sub(a, b):
        return a[0] - b[0], a[1] - b[1]

    even, odd = add(x[0], x[2]), add(x[1], x[3])
    left, across = sub(x[0], x[2]), sub(x[1], x[3])
    return (
        add(even, odd),
        (left[0] - across[1], left[1] + across[0]),
        sub(even, odd),
        (left[0] + across[1], left[1] - across[0]),
    )


def wrapped(x, length):
    return jnp.where(x >= length, x - length, x)


def wait_bytes(ref, sem):
    pltpu.make_async_copy(ref, ref, sem).wait()


def kernel(
    cells, blocks, occ, vir, out_0, out_1,
    cells_v, occ_v, blocks_v, pos_v, pos_s,
    sent_half_0, sent_half_1, sent_rest, got_half_0, got_half_1, got_rest,
    middle, middle_rest, whole_rest, sent_spec, sent_spec_rest, got_spec_0, got_spec_1, got_rest_0, got_rest_1,
    vir_own, vir_sent, vir_all, vir_high, vir_low, rest_high, rest_low, band, sent_pairs,
    load_sem, pos_sem, half_send, half_recv, half_local, spec_send, spec_recv, spec_local,
    pair_send, pair_recv, pair_local, vir_load_sem, vir_send, vir_recv, vir_local,
):
    me = lax.axis_index("cell")
    my_aux = lax.axis_index("aux")
    partner = my_aux + 1 - 2 * lax.rem(my_aux, 2)
    active = lax.rem(me, GROUP) != GROUP - 1
    my_slot = me - me // GROUP
    out = (out_0, out_1)
    sent_half = (sent_half_0, sent_rest, sent_half_1)
    got_half = (got_half_0, got_rest, got_half_1)
    got_spec = (got_spec_0, got_spec_1)
    got_spec_rest = (got_rest_0, got_rest_1)
    my_low, my_side = lax.rem(me, SIDE), me // SIDE
    my_block = me // GROUP
    my_first = wrapped(lax.rem(me, GROUP), GROUP - 1)
    share_at, share_start = [], []
    for g in range(2):
        place = wrapped(me + CELLS - GROUP * g, CELLS)
        share_at.append(lax.rem(place, SIDE))
        share_start.append(GROUP * g + place // SIDE * SIDE)

    def for_members(g, send):
        def at(offset):
            u = wrapped(share_at[g] + offset, SIDE)
            send(wrapped(share_start[g] + u, CELLS), u)

        def one(j, carry):
            at(SIDE // 2 - j)
            at(SIDE // 2 + j)
            return carry

        at(SIDE // 2)
        lax.fori_loop(1, SIDE // 2, one, 0)

    def share_slot(g):
        return lax.rem(my_slot + WORKERS - (GROUP - 1) * g, SHARE)

    occ_loads = [pltpu.make_async_copy(occ.at[:, t, :], occ_v.at[t], load_sem.at[t]) for t in range(2)]
    block_loads = [pltpu.make_async_copy(blocks.at[:, p, :], blocks_v.at[p], load_sem.at[2 + p]) for p in range(ROWS)]
    vir_load = pltpu.make_async_copy(vir, vir_own, vir_load_sem)
    cells_load = pltpu.make_async_copy(cells, cells_v, pos_sem)
    cells_load.start()
    vir_load.start()
    for load in occ_loads + block_loads:
        load.start()


    barrier = pltpu.get_barrier_semaphore()

    def greet(j, carry):
        for offset in (SIDE - j, SIDE + j):
            pl.semaphore_signal(
                barrier, inc=1, device_id={"cell": wrapped(me + offset, CELLS)}, device_id_type=MESH
            )
        return carry

    def greet_aux(j, carry):
        pl.semaphore_signal(
            barrier, inc=1, device_id={"aux": lax.rem(my_aux + 2 * j, AUX)}, device_id_type=MESH
        )
        return carry

    pl.semaphore_signal(barrier, inc=1, device_id={"cell": wrapped(me + SIDE, CELLS)}, device_id_type=MESH)
    for j in range(1, SIDE):
        greet(j, 0)
    lax.fori_loop(1, AUX // 2, greet_aux, 0)
    pl.semaphore_signal(barrier, inc=1, device_id={"aux": partner}, device_id_type=MESH)

    cells_load.wait()
    folded = cells_v[...] & 3
    number = folded[0:1] * 16 + folded[1:2] * 4 + folded[2:3]
    wanted = lax.broadcasted_iota(jnp.int32, (CELLS, CELLS), 0)
    holder = lax.broadcasted_iota(jnp.int32, (CELLS, CELLS), 1)
    found = jnp.sum(jnp.where(number == wanted, holder, 0), axis=1, keepdims=True)
    pos_v[...] = jnp.broadcast_to(found & (CELLS - 1), (CELLS, LANES))
    pos_copy = pltpu.make_async_copy(pos_v, pos_s, pos_sem)
    pos_copy.start()

    def vir_slot(side, aux):
        return vir_all.at[side, :, pl.ds(aux * PIECE, PIECE)]

    def vir_copy(source, side, aux, target, sem):
        return pltpu.make_async_remote_copy(
            src_ref=source,
            dst_ref=vir_slot(side, aux),
            send_sem=vir_send.at[sem],
            recv_sem=vir_recv.at[sem],
            device_id=target,
            device_id_type=MESH,
        )

    def spread_vir(source, side):
        def one(j, carry):
            vir_copy(source, side, my_aux, {"aux": lax.rem(my_aux + 2 * j, AUX)}, 0).start()
            return carry

        lax.fori_loop(1, AUX // 2, one, 0)
        vir_copy(source, side, my_aux, {"aux": partner}, 1).start()

    vir_load.wait()
    shut = jnp.zeros((PIECE, HALF - REST), F32)
    for t in range(2):
        for n in range(2):
            vir_sent[n * 2 + t, :, 0, :] = vir_own[:, t, n * LANES : (n + 1) * LANES]
    vir_sent[STRIPS - 1, :, 0, :] = jnp.concatenate(
        [vir_own[:, 0, WIDE:NB], shut, vir_own[:, 1, WIDE:NB], shut], axis=1
    )
    pl.semaphore_wait(barrier, CELLS - 1 + AUX // 2)
    vir_copy(vir_sent, my_side, my_aux, {"cell": lax.rem(me + SIDE, CELLS)}, 2).start()
    spread_vir(vir_sent, my_side)
    own_vir = pltpu.make_async_copy(vir_sent, vir_slot(my_side, my_aux), vir_local)
    own_vir.start()

    for load in occ_loads:
        load.wait()
    blank = jnp.zeros((SLOTS - NO, NB), F32)
    left = split(jnp.concatenate([occ_v[0], blank, -occ_v[1], blank], axis=0))

    def half_product(pair):
        for load in block_loads[2 * pair : 2 * pair + 2]:
            load.wait()
        for at in range(2):
            product = dot3(left, split(blocks_v[2 * pair + at, :, 0:WIDE]))
            for t in range(2):
                for n in range(2):
                    rows = product[t * SLOTS : t * SLOTS + NO, n * LANES : (n + 1) * LANES]
                    sent_half[2 * pair][pl.ds(t * 4 + n * 2 + at, NO, stride=8), :] = rows

    def rest_product():
        gap = jnp.zeros((NB, HALF - REST), F32)
        parts = []
        for at in range(2):
            for pair in range(2):
                parts += [blocks_v[2 * pair + at, :, WIDE:NB], gap]
        product = dot3(left, split(jnp.concatenate(parts, axis=1)))
        for t in range(2):
            for at in range(2):
                sent_rest[:, t * 2 + at, :] = product[t * SLOTS : t * SLOTS + NO, at * LANES : (at + 1) * LANES]

    def half_source(part, slot):
        if part == SMALL:
            return sent_rest.at[slot]
        return sent_half[part].at[pl.ds(pl.multiple_of(slot * 8, 8), 8)]

    def send_half(part):
        for turn in (2, 3, 1, 0):
            block = wrapped(my_block + turn, 4)

            def one(j, carry):
                m = wrapped(j + my_first, GROUP - 1)
                peer = block * GROUP + m

                def send():
                    pltpu.make_async_remote_copy(
                        src_ref=half_source(part, block * (GROUP - 1) + m),
                        dst_ref=got_half[part].at[me],
                        send_sem=half_send.at[part],
                        recv_sem=half_recv.at[part],
                        device_id={"cell": peer},
                        device_id_type=MESH,
                    ).start()

                if turn:
                    send()
                else:
                    pl.when(peer != me)(send)
                return carry

            lax.fori_loop(0, GROUP - 1, one, 0)

        @pl.when(active)
        def _():
            pltpu.make_async_copy(half_source(part, my_slot), got_half[part].at[me], half_local.at[part]).start()

    half_product(0)
    send_half(FIRST)

    half_product(1)
    rest_product()
    send_half(SMALL)
    send_half(SECOND)

    pos_copy.wait()
    first_half = lax.broadcasted_iota(jnp.int32, (2, LANES), 1) < HALF
    sign = jnp.where(lax.broadcasted_iota(jnp.int32, (8, LANES), 0) < ROWS, -1.0, 1.0).astype(F32)

    def spec_copy(part, g):
        if part == SMALL:
            return sent_spec_rest.at[g], got_spec_rest[g].at[share_slot(g)], 2 + g
        return sent_spec.at[g], got_spec[g].at[:, pl.ds(pl.multiple_of(share_slot(g) * 8, 8), 8)], g

    def arrived_half(part):
        wait_bytes(got_half[part].at[pl.ds(0, CELLS - 1)], half_recv.at[part])
        wait_bytes(got_half[part].at[0], half_local.at[part])

    def send_spec(part, g):
        sources, target, sem = spec_copy(part, g)

        def send(peer, u):
            pltpu.make_async_remote_copy(
                src_ref=sources.at[wrapped(peer, SIDE)],
                dst_ref=target,
                send_sem=spec_send.at[sem],
                recv_sem=spec_recv.at[sem],
                device_id={"cell": peer},
                device_id_type=MESH,
            ).start()

        for_members(g, send)
        pltpu.make_async_copy(sources.at[my_low], target, spec_local.at[sem]).start()

    def fourier(part):
        arrived_half(part)
        for c in range(4):
            x = [[got_half[part][pos_s[a * 16 + b * 4 + c, 0]] for b in range(4)] for a in range(4)]
            columns = [four_points([x[a][b] for a in range(4)], sign) for b in range(4)]
            for a in range(4):
                y = four_points([columns[b][a] for b in range(4)], sign)
                for b in range(4):
                    middle[a * 16 + b * 4 + c] = y[b]
        for at in range(16):
            y = four_points([middle[at * 4 + c] for c in range(4)], sign)
            for c in range(4):
                k = at * 4 + c
                sent_spec[part // 2, k % SIDE, k // SIDE] = y[c]
        send_spec(part, part // 2)

    def fourier_rest():
        arrived_half(SMALL)
        for c in range(4):
            x = [[None] * 4 for _ in range(4)]
            for a in range(4):
                for b in range(4):
                    both = got_rest[pos_s[a * 16 + b * 4 + c, 0]]
                    x[a][b] = (both[0:2], both[2:4])
            columns = [four_complex([x[a][b] for a in range(4)]) for b in range(4)]
            for a in range(4):
                y = four_complex([columns[b][a] for b in range(4)])
                for b in range(4):
                    for t in range(2):
                        middle_rest[a * 16 + b * 4 + c, 2 * t : 2 * t + 2] = y[b][t]
        for at in range(16):
            x = [(middle_rest[at * 4 + c, 0:2], middle_rest[at * 4 + c, 2:4]) for c in range(4)]
            y = four_complex(x)
            for c in range(4):
                for t in range(2):
                    whole_rest[at * 4 + c, 2 * t : 2 * t + 2] = y[c][t]
        for k in range(SIDE):
            for t in range(2):
                rows = slice(2 * t, 2 * t + 2)
                low, high = whole_rest[k, rows], whole_rest[k + SIDE, rows]
                sent_spec_rest[0, k, rows] = jnp.where(first_half, low, pltpu.roll(high, HALF, 1))
                sent_spec_rest[1, k, rows] = jnp.where(first_half, pltpu.roll(low, HALF, 1), high)
        for g in range(2):
            send_spec(SMALL, g)

    other = 1 - my_side
    wait_bytes(vir_slot(0, 0), vir_recv.at[2])
    spread_vir(vir_slot(other, my_aux), other)

    @pl.when(active)
    def _():
        fourier(FIRST)
        fourier_rest()
        fourier(SECOND)

    wait_bytes(vir_all.at[:, :, pl.ds(0, NV // 2 - PIECE)], vir_recv.at[0])

    def hand_on(j, carry):
        source = lax.rem(my_aux + 2 * j, AUX)
        for side in range(2):
            vir_copy(vir_slot(side, source), side, source, {"aux": partner}, 1).start()
        return carry

    lax.fori_loop(1, AUX // 2, hand_on, 0)
    own_vir.wait()
    wait_bytes(vir_all.at[:, :, pl.ds(0, NV // 2)], vir_recv.at[1])
    none = jnp.zeros((NV, HALF), F32)
    for side in range(2):
        rest = vir_all[side, STRIPS - 1, :, 0, :]
        for t in range(2):
            for n in range(2):
                high, low = split(vir_all[side, n * 2 + t, :, 0, :])
                at = t * WIDE + n * LANES
                vir_high[side, :, at : at + LANES] = high
                vir_low[side, :, at : at + LANES] = low
            small = rest[:, t * HALF : (t + 1) * HALF]
            high, low = split(jnp.concatenate([none, small] if side else [small, none], axis=1))
            rest_high[side, :, t * LANES : (t + 1) * LANES] = high
            rest_low[side, :, t * LANES : (t + 1) * LANES] = low

    def spec_bytes(part, g, count):
        if part == SMALL:
            return got_spec_rest[g].at[pl.ds(0, count)]
        return got_spec[g].at[:, pl.ds(0, count * 8)]

    def arrived_spec(part, g):
        sem = spec_copy(part, g)[2]

        @pl.when(active)
        def _():
            wait_bytes(spec_bytes(part, g, SHARE - 1), spec_recv.at[sem])
            wait_bytes(spec_bytes(part, g, 1), spec_local.at[sem])

        @pl.when(jnp.logical_not(active))
        def _():
            wait_bytes(spec_bytes(part, g, SHARE), spec_recv.at[sem])

    def turned(even, odd):
        upper = jnp.concatenate(even + [-x for x in odd], axis=1)
        lower = jnp.concatenate(odd + even, axis=1)
        return [upper, lower]

    lane = lax.broadcasted_iota(jnp.int32, (ROWS, WIDE), 1)

    def band_and_pairs(g):
        arrived_spec(2 * g, g)
        arrived_spec(SMALL, g)
        for side in range(2):
            main, small = [], []
            for at in range(2):
                x = [
                    [got_spec[g][side, pl.ds(t * 4 + n * 2 + at, SIDE, stride=8), :] for n in range(2)]
                    for t in range(2)
                ]
                main += turned(x[0], x[1])
                y = [got_spec_rest[g][:, t * 2 + at, :] for t in range(2)]
                small += turned([y[0]], [y[1]])
            value = dot3(split(jnp.concatenate(main, axis=0)), (vir_high[side], vir_low[side]), transposed=True)
            value = value + dot3(split(jnp.concatenate(small, axis=0)), (rest_high[side], rest_low[side]), transposed=True)
            value = jnp.concatenate([value, jnp.zeros((4 * SIDE, WIDE - NV), F32)], axis=1)
            for at in range(2):
                for t in range(2):
                    start = (at * 2 + t) * SIDE
                    for n in range(2):
                        band[g, side, n, pl.ds(t * 2 + at, SHARE, stride=4), :] = value[
                            start : start + SHARE, n * LANES : (n + 1) * LANES
                        ]

        for block in range(2):
            base = block * (GROUP - 1)
            for side in range(2):

                def wide(i):
                    return jnp.concatenate([band[g, side, n, 4 * i : 4 * i + 4, :] for n in range(2)], axis=1)

                for m in range(GROUP):
                    shift = (NV - PAIRS) * m
                    if m == 0:
                        chunk = wide(base)
                    else:
                        chunk = pltpu.roll(wide(base + m - 1), WIDE - (NV - shift), 1)
                        if m < GROUP - 1:
                            chunk = jnp.where(lane < shift, chunk, pltpu.roll(wide(base + m), shift, 1))
                    sent_pairs[g, block * GROUP + m, side] = chunk

        def send(peer, u):
            pltpu.make_async_remote_copy(
                src_ref=sent_pairs.at[g, u],
                dst_ref=out[g].at[my_low],
                send_sem=pair_send.at[g],
                recv_sem=pair_recv.at[g],
                device_id={"cell": peer},
                device_id_type=MESH,
            ).start()

        for_members(g, send)
        pltpu.make_async_copy(sent_pairs.at[g, share_at[g]], out[g].at[my_low], pair_local.at[g]).start()

    for g in range(2):
        band_and_pairs(g)

    for part in (FIRST, SMALL, SECOND):
        step = 1 if part == SMALL else 8

        @pl.when(active)
        def _():
            wait_bytes(sent_half[part].at[pl.ds(0, (WORKERS - 1) * step)], half_send.at[part])

        @pl.when(jnp.logical_not(active))
        def _():
            wait_bytes(sent_half[part].at[pl.ds(0, WORKERS * step)], half_send.at[part])

    @pl.when(active)
    def _():
        for g in range(2):
            wait_bytes(sent_spec.at[g, pl.ds(0, SIDE - 1)], spec_send.at[g])
            wait_bytes(sent_spec_rest.at[g, pl.ds(0, SIDE - 1)], spec_send.at[2 + g])

    wait_bytes(vir_all.at[:, :, pl.ds(0, NV // 2 - PIECE)], vir_send.at[0])
    wait_bytes(vir_all.at[:, :, pl.ds(0, NV // 2)], vir_send.at[1])
    wait_bytes(vir_slot(0, 0), vir_send.at[2])
    for g in range(2):
        wait_bytes(sent_pairs.at[g, pl.ds(0, SIDE - 1)], pair_send.at[g])
        wait_bytes(out[g].at[0], pair_local.at[g])
        wait_bytes(out[g].at[pl.ds(0, SIDE - 1)], pair_recv.at[g])


def exchange(cells, blocks, occ, vir):
    dma = pltpu.SemaphoreType.DMA
    pairs = jax.ShapeDtypeStruct((SIDE, 2, ROWS, WIDE), F32)
    tiles = pltpu.VMEM((CELLS, 8, LANES), F32)
    halves = pltpu.VMEM((SLOTS, 4, LANES), F32)
    return pl.pallas_call(
        kernel,
        out_shape=(pairs, pairs),
        in_specs=[
            pl.BlockSpec(memory_space=pl.ANY),
            pl.BlockSpec(memory_space=pl.ANY),
            pl.BlockSpec(memory_space=pl.ANY),
            pl.BlockSpec(memory_space=pl.ANY),
        ],
        out_specs=(pl.BlockSpec(memory_space=pltpu.VMEM), pl.BlockSpec(memory_space=pltpu.VMEM)),
        scratch_shapes=[
            pltpu.VMEM((3, CELLS), jnp.int32),
            pltpu.VMEM((2, NO, NB), F32),
            pltpu.VMEM((ROWS, NB, NB), F32),
            pltpu.VMEM((CELLS, LANES), jnp.int32),
            pltpu.SMEM((CELLS, LANES), jnp.int32),
            pltpu.VMEM((WORKERS * 8, LANES), F32),
            pltpu.VMEM((WORKERS * 8, LANES), F32),
            pltpu.VMEM((WORKERS, 4, LANES), F32),
            tiles,
            tiles,
            halves,
            tiles,
            halves,
            halves,
            pltpu.VMEM((2, SIDE, 2, 8, LANES), F32),
            pltpu.VMEM((2, SIDE, 4, LANES), F32),
            pltpu.VMEM((2, SIDE * 8, LANES), F32),
            pltpu.VMEM((2, SIDE * 8, LANES), F32),
            pltpu.VMEM((SIDE, 4, LANES), F32),
            pltpu.VMEM((SIDE, 4, LANES), F32),
            pltpu.VMEM((PIECE, 2, NB), F32),
            pltpu.VMEM((STRIPS, PIECE, 1, LANES), F32),
            pltpu.VMEM((2, STRIPS, NV, 1, LANES), F32),
            pltpu.VMEM((2, NV, 2 * WIDE), BF16),
            pltpu.VMEM((2, NV, 2 * WIDE), BF16),
            pltpu.VMEM((2, NV, WIDE), BF16),
            pltpu.VMEM((2, NV, WIDE), BF16),
            pltpu.VMEM((2, 2, 2, SHARE * 4, LANES), F32),
            pltpu.VMEM((2, SIDE, 2, ROWS, WIDE), F32),
            dma((2 + ROWS,)),
            dma,
            dma((3,)),
            dma((3,)),
            dma((3,)),
            dma((4,)),
            dma((4,)),
            dma((4,)),
            dma((2,)),
            dma((2,)),
            dma((2,)),
            dma,
            dma((3,)),
            dma((3,)),
            dma,
        ],
        compiler_params=pltpu.CompilerParams(
            collective_id=0, has_side_effects=True, vmem_limit_bytes=44 << 20
        ),
        name="transform",
    )(cells, blocks, occ, vir)


def reorder_kernel(transfer, got_0, got_1, out, rows, ordered, sem):
    first = transfer[0]
    shifts = (first // 16, first // 4 % 4, first % 4)
    along = [[(n - shift) & 3 for n in range(4)] for shift in shifts]
    copies = []
    for g, got in enumerate((got_0, got_1)):
        for q in range(CELLS):
            source = along[0][q // 16] * 16 + along[1][q // 4 % 4] * 4 + along[2][q % 4]
            tile = got[source & (SIDE - 1), source >> 5]
            for t in range(2):
                for n in range(2):
                    at = (t * ROWS + 2 * g) * CELLS + q
                    rows[n, pl.ds(at, 2, stride=CELLS), :] = tile[2 * t : 2 * t + 2, n * LANES : (n + 1) * LANES]
        for t in range(2):
            for p in (2 * g, 2 * g + 1):
                at = (t * ROWS + p) * CELLS
                ordered[t, p, :, 0:LANES] = rows[0, at : at + CELLS, :]
                ordered[t, p, :, LANES:PAIRS] = rows[1, at : at + CELLS, 0 : PAIRS - LANES]
            both = pl.ds(2 * g, 2)
            copy = pltpu.make_async_copy(ordered.at[t, both], out.at[t, both], sem.at[g, t])
            copy.start()
            copies.append(copy)
    for copy in copies:
        copy.wait()


def reorder(transfer, got_0, got_1):
    whole = pl.BlockSpec(memory_space=pltpu.VMEM)
    return pl.pallas_call(
        reorder_kernel,
        out_shape=jax.ShapeDtypeStruct((2, ROWS, CELLS, PAIRS), F32),
        in_specs=[pl.BlockSpec(memory_space=pltpu.SMEM), whole, whole],
        out_specs=pl.BlockSpec(memory_space=pl.ANY),
        scratch_shapes=[
            pltpu.VMEM((2, 2 * ROWS * CELLS, LANES), F32),
            pltpu.VMEM((2, ROWS, CELLS, PAIRS), F32),
            pltpu.SemaphoreType.DMA((2, 2)),
        ],
        compiler_params=pltpu.CompilerParams(vmem_limit_bytes=16 << 20),
        name="reorder",
    )(transfer, got_0, got_1)


def on_device(blocks, cell_offsets, occ_coeff, vir_coeff, transfer_index):
    keep = functools.partial(pltpu.with_memory_space_constraint, memory_space=pltpu.HBM)
    got = exchange(
        keep(cell_offsets),
        keep(jnp.transpose(blocks[0], (1, 0, 2))),
        keep(jnp.transpose(occ_coeff, (2, 0, 1))),
        keep(jnp.transpose(vir_coeff[0], (2, 0, 1))),
    )
    return reorder(transfer_index, *got)


def solution(mesh):
    placed = (P("cell", "aux", None, None), P(), P(), P("cell", None, None, "aux"), P())
    return jax.shard_map(
        on_device,
        mesh=mesh,
        in_specs=placed,
        out_specs=P(None, "aux", None, "cell"),
        check_vma=False,
    )
```
